512 devices in a mesh: dp: 16 (over z), pipe: 4 (over x), tensor: 8 (over y, core).
Axes of the slice: x: 4, y: 4, z: 16, core: 2. Of those that a mesh axis runs over, the one named last changes fastest.
Arguments:
- tokens: bfloat16 [16384, 8192], P('dp', ('pipe', 'tensor')), may hold values from -6 to 6
- key_value_weight: bfloat16 [8192, 2048], P(('pipe', 'tensor')), may hold values from -0.0625 to 0.0625
- adapter_down: bfloat16 [96, 8192, 128], P(None, ('pipe', 'tensor', 'dp')), may hold values from -0.0625 to 0.0625
- adapter_up: bfloat16 [96, 64, 2048], P(None, 'dp'), may hold values from -0.75 to 0.75
- tenant_of_block: int32 [128], replicated, may hold values from 0 to 95
- slot_of_tenant: int32 [96], replicated, may hold values from 0 to 95, each once
- cotangent: bfloat16 [16384, 2048], P(('dp', 'pipe', 'tensor')), may hold values from -1.5 to 1.5
Outputs:
- key_value: bfloat16 [16384, 2048], P(('dp', 'pipe', 'tensor'))
- input_grad: bfloat16 [16384, 8192], P('dp', ('pipe', 'tensor'))
- grad_a: float32 [96, 8192, 128], P(None, ('pipe', 'tensor', 'dp'))
- grad_b: float32 [96, 64, 2048], P(None, 'dp', ('pipe', 'tensor'))
The draws below stay inside these ranges and needn't reach their ends.
Inputs may be any that keep to these rules, and one draw needn't show every extreme that they name: `slot_of_tenant`: each slot holds exactly one tenant.
All inputs are finite; a program needn't handle non-finite values.
Results may differ from the reference program's by a relative error of at most 0.017.
Values may be sent and summed in bfloat16 or wider, within the bound.
A program may use at most 64 MiB of HBM per device.

```python
import math
import jax
import jax.numpy as jnp
import numpy as np
from jax import lax

MODEL_WIDTH = 8192
KEY_WIDTH = 1024
ADAPTER_RANK = 64
BLOCK = 128
TENANT_COUNT = 96
TOKENS = 16384
BLOCKS = 128
N_PIPE = 4
N_TENSOR = 8


def with_ends(array, key, low, largest):
    extent = array.shape
    index_at = [jax.random.randint(jax.random.fold_in(key, axis), (), 0, extent[axis]) for axis in range(len(extent))]
    array = array.at[tuple(index_at)].set(low)
    longest = extent.index(max(extent))
    index_at[longest] = (index_at[longest] + 1) % extent[longest]
    return array.at[tuple(index_at)].set(largest)


def with_spikes(values, rng, source, target, shards_of, factor):
    owner, partner = [(jnp.arange(values.shape[axis_at]) // (values.shape[axis_at] // shards_of)).reshape([-1 if axis == axis_at else 1 for axis in range(values.ndim)]) for axis_at in (source, target)]
    chosen = jax.random.permutation(rng, shards_of)[partner]
    strong = (owner == chosen) | (owner == (partner + shards_of // 2) % shards_of)
    return jnp.where(strong, factor * values, values)


def levels(rng, dims, cuts, smallest, high):
    factor_of, own = 1.0, jax.random.fold_in(rng, 6)
    for position, blocks in cuts:
        heights = jnp.exp(jax.random.uniform(jax.random.fold_in(own, position), (blocks,), jnp.float32, smallest / len(cuts), high / len(cuts)))
        factor_of = factor_of * jnp.repeat(heights, dims[position] // blocks).reshape([-1 if axis == position else 1 for axis in range(len(dims))])
    return factor_of


def rank_table(count, lean):
    weights = [(1 << 20) // math.isqrt(standing ** lean) + 1 for standing in range(1, count + 1)]
    spread = 1 + sum(weights) // (1 << 30)
    return np.cumsum(np.array([max(1, weight // spread) for weight in weights]))


def ranked_ids(rng, extent, count, lean):
    listing = rank_table(count, lean)
    pick = jax.random.randint(jax.random.fold_in(rng, 1), extent, 0, int(listing[count - 1]))
    standing = jnp.searchsorted(jnp.asarray(listing, jnp.int32), pick, side="right")
    return jax.random.permutation(jax.random.fold_in(rng, 2), count)[standing].astype(jnp.int32)


def gaussian(own_key, dims, scale, bound, split=(), held_as=jnp.bfloat16):
    values = jax.random.normal(own_key, dims, jnp.float32) * scale
    if len(split) > 0:
        values = levels(own_key, dims, split, -0.22, 0.18) * values
    return jnp.clip(values, min=-bound, max=bound).astype(held_as)


def bell_draw_with(rng, dims, scale, limit, split, heavy, kind=jnp.bfloat16):
    result = scale * jax.random.normal(rng, dims, jnp.float32)
    if split:
        result = result * levels(rng, dims, split, -0.22, 0.18)
    return jnp.clip(with_spikes(result, jax.random.fold_in(rng, 3), *heavy), -limit, limit).astype(kind)


def setup_inputs(seed: int = 0) -> dict:
    keys = jax.random.split(jax.random.key(seed), 8)
    return {
        "tokens": bell_draw_with(keys[0], (TOKENS, MODEL_WIDTH), 1.0, 6.0, ((0, 16), (1, 32)), (1, 0, 32, 2.75)),
        "key_value_weight": gaussian(keys[1], (MODEL_WIDTH, 2 * KEY_WIDTH), MODEL_WIDTH ** -0.5, 0.0625, ((0, 32),)),
        "adapter_down": gaussian(keys[2], (TENANT_COUNT, MODEL_WIDTH, 2 * ADAPTER_RANK), MODEL_WIDTH ** -0.5, 0.0625, ((1, 512),)),
        "adapter_up": gaussian(keys[3], (TENANT_COUNT, ADAPTER_RANK, 2 * KEY_WIDTH), ADAPTER_RANK ** -0.5, 0.75, ((1, 16),)),
        "tenant_of_block": with_ends(ranked_ids(keys[4], (BLOCKS,), TENANT_COUNT, 2), jax.random.fold_in(keys[4], 3), 0, TENANT_COUNT - 1).astype(jnp.int32),
        "slot_of_tenant": jax.random.permutation(keys[5], TENANT_COUNT).astype(jnp.int32),
        "cotangent": gaussian(keys[6], (TOKENS, 2 * KEY_WIDTH), 0.25, 1.5, ((0, 512),)),
    }


def reference(tokens, key_value_weight, adapter_down, adapter_up, tenant_of_block, slot_of_tenant, cotangent):
    group_total = N_PIPE * N_TENSOR
    feature_count = MODEL_WIDTH // group_total
    token_count = tokens.shape[0]
    block_count = token_count // BLOCK
    slot_of_block = slot_of_tenant[tenant_of_block].astype(jnp.int32)
    down_blocks = adapter_down[slot_of_block]
    up_blocks = adapter_up[slot_of_block]

    def one_group(totals, group_index):
        base_sum, low_sum = totals
        first_col = group_index * feature_count
        x_piece = lax.dynamic_slice_in_dim(tokens, first_col, feature_count, 1)
        w_piece = lax.dynamic_slice_in_dim(key_value_weight, first_col, feature_count, 0)
        base_piece = jnp.dot(x_piece, w_piece, preferred_element_type=jnp.float32).astype(jnp.bfloat16)
        base_piece = lax.optimization_barrier(base_piece).astype(jnp.float32)
        a_piece = lax.dynamic_slice_in_dim(down_blocks, first_col, feature_count, 1)
        low_piece = jnp.einsum('bif,bfr->bir', x_piece.reshape(block_count, BLOCK, feature_count).astype(jnp.float32), a_piece.astype(jnp.float32))
        low_piece = lax.optimization_barrier(low_piece.astype(jnp.bfloat16)).astype(jnp.float32)
        return (base_sum + base_piece, low_sum + low_piece), None

    start_totals = (jnp.zeros((token_count, 2 * KEY_WIDTH), jnp.float32), jnp.zeros((block_count, BLOCK, 2 * ADAPTER_RANK), jnp.float32))
    (base_sum, low_sum), _ = lax.scan(one_group, start_totals, jnp.arange(group_total, dtype=jnp.int32))
    low_float = lax.optimization_barrier(low_sum.astype(jnp.bfloat16)).astype(jnp.float32)
    b_float = up_blocks.astype(jnp.float32)
    lowrank = jnp.concatenate([
        jnp.einsum('bir,brc->bic', low_float[..., :ADAPTER_RANK], b_float[..., :KEY_WIDTH]),
        jnp.einsum('bir,brc->bic', low_float[..., ADAPTER_RANK:], b_float[..., KEY_WIDTH:])], axis=2)
    key_value = (base_sum + lowrank.reshape(token_count, 2 * KEY_WIDTH)).astype(jnp.bfloat16)

    cot_blocks = cotangent.reshape(block_count, BLOCK, 2 * KEY_WIDTH).astype(jnp.float32)
    low_grad = jnp.concatenate([
        jnp.einsum('bic,brc->bir', cot_blocks[..., :KEY_WIDTH], b_float[..., :KEY_WIDTH]),
        jnp.einsum('bic,brc->bir', cot_blocks[..., KEY_WIDTH:], b_float[..., KEY_WIDTH:])], axis=2)
    low_grad = lax.optimization_barrier(low_grad.astype(jnp.bfloat16)).astype(jnp.float32)
    input_grad = jnp.dot(cotangent, key_value_weight.T, preferred_element_type=jnp.float32)
    input_grad = input_grad + jnp.einsum('bir,bfr->bif', low_grad, down_blocks.astype(jnp.float32)).reshape(token_count, MODEL_WIDTH)
    input_grad = input_grad.astype(jnp.bfloat16)

    tok_blocks = tokens.reshape(block_count, BLOCK, MODEL_WIDTH).astype(jnp.float32)
    grad_a_blocks = jnp.einsum('bif,bir->bfr', tok_blocks, low_grad)
    grad_a = jax.ops.segment_sum(grad_a_blocks, slot_of_block, num_segments=TENANT_COUNT)
    grad_b_blocks = jnp.concatenate([
        jnp.einsum('bir,bic->brc', low_float[..., :ADAPTER_RANK], cot_blocks[..., :KEY_WIDTH]),
        jnp.einsum('bir,bic->brc', low_float[..., ADAPTER_RANK:], cot_blocks[..., KEY_WIDTH:])], axis=2)
    grad_b = jax.ops.segment_sum(grad_b_blocks, slot_of_block, num_segments=TENANT_COUNT)
    return (key_value, input_grad, grad_a, grad_b)
```

```python
import functools

import jax
import jax.numpy as jnp
from jax import lax
from jax.experimental import pallas as pl
from jax.experimental.pallas import tpu as pltpu
from jax.sharding import PartitionSpec as P

MESH = pl.DeviceIdType.MESH
F32, BF16, I32 = jnp.float32, jnp.bfloat16, jnp.int32
NZ, NX, NY = 16, 4, 4
SLOTS, UP, DOWN, RANKS = 96, 4, 16, 128
BLOCKS = 8
ROWS, FEATS, WIDTH, HALF, QUARTER = 32, 256, 2048, 1024, 512
COLS = 64


def scratches():
    return dict(
        au=pltpu.VMEM((SLOTS, UP, WIDTH), BF16),
        ad=pltpu.VMEM((SLOTS, DOWN, RANKS), BF16),
        xv=pltpu.VMEM((NX, NY, 2, ROWS, FEATS), BF16),
        wv=pltpu.VMEM((FEATS, WIDTH), BF16),
        xp=pltpu.VMEM((NX, NY, ROWS, FEATS), BF16),
        wp=pltpu.VMEM((FEATS, WIDTH), BF16),
        bsend=pltpu.VMEM((NZ, UP, QUARTER), BF16),
        brecv=pltpu.VMEM((NZ, UP, QUARTER), BF16),
        bqf=pltpu.VMEM((NZ * UP, QUARTER), F32),
        bown=pltpu.VMEM((4, NZ * UP, QUARTER), BF16),
        asend=pltpu.VMEM((NZ, BLOCKS, DOWN, RANKS), BF16),
        arecv=pltpu.VMEM((NZ, BLOCKS, DOWN, RANKS), BF16),
        c0=pltpu.VMEM((NX, NY, 2, ROWS, HALF), BF16),
        c1=pltpu.VMEM((NX, NY, 2, ROWS, HALF), BF16),
        pa=pltpu.VMEM((NX, NY, ROWS, HALF), BF16),
        pb=pltpu.VMEM((NY, NX, ROWS, HALF), BF16),
        ra1=pltpu.VMEM((3, NY, ROWS, HALF), BF16),
        rb1=pltpu.VMEM((3, NX, ROWS, HALF), BF16),
        qa=pltpu.VMEM((NY, ROWS, HALF), BF16),
        qb=pltpu.VMEM((NX, ROWS, HALF), BF16),
        ra2=pltpu.VMEM((3, ROWS, HALF), BF16),
        rb2=pltpu.VMEM((3, ROWS, HALF), BF16),
        lg=pltpu.VMEM((NX, NY, 2, ROWS, RANKS), BF16),
        lp=pltpu.VMEM((NX, NY, 2, ROWS, RANKS), BF16),
        lr=pltpu.VMEM((7, NY, ROWS, RANKS), BF16),
        lq=pltpu.VMEM((NY, ROWS, RANKS), BF16),
        ls=pltpu.VMEM((3, ROWS, RANKS), BF16),
        la=pltpu.VMEM((NX, NY, 2, ROWS, RANKS), BF16),
        gasend=pltpu.VMEM((NZ, BLOCKS, DOWN, RANKS), BF16),
        garecv=pltpu.VMEM((NZ, BLOCKS, DOWN, RANKS), BF16),
        gbf=pltpu.VMEM((NZ, DOWN, RANKS), F32),
        gbsend=pltpu.VMEM((NZ, DOWN, RANKS), BF16),
        gbrecv=pltpu.VMEM((NZ, DOWN, RANKS), BF16),
        tga=pltpu.VMEM((NZ, 1, RANKS), I32),
        tgb=pltpu.VMEM((2, 1, NZ * DOWN), I32),
        gaacc=pltpu.VMEM((SLOTS * DOWN, RANKS), F32),
        gbt=pltpu.VMEM((UP, COLS, SLOTS), F32),
        igv=pltpu.VMEM((NX, NY * 2 * ROWS, FEATS), BF16),
        kvv=pltpu.VMEM((ROWS, WIDTH), BF16),
        loc=pltpu.SemaphoreType.DMA((12,)),
        zs=pltpu.SemaphoreType.DMA((4, NZ)),
        zr=pltpu.SemaphoreType.DMA((4, NZ)),
        ps=pltpu.SemaphoreType.DMA((80,)),
        pr=pltpu.SemaphoreType.DMA((80,)),
    )


def kern(names, ten, slot, x_h, w_h, ad_h, au_h, cot_h, kv_o, ig_o, ga_o, gb_o, *refs):
    s = dict(zip(names, refs, strict=True))
    z, x, t = lax.axis_index("dp"), lax.axis_index("pipe"), lax.axis_index("tensor")
    y, c = lax.div(t, 2), lax.rem(t, 2)
    own_block = x * 2 + lax.div(y, 2)
    quarter = lax.rem(t, 4)

    locals_ = {}

    def local(name, src, dst, i):
        cp = pltpu.make_async_copy(src, dst, s["loc"].at[i])
        cp.start()
        locals_[name] = cp

    local("au", au_h, s["au"], 0)
    local("ad", ad_h, s["ad"], 1)
    local("c0", cot_h.at[:, pl.ds(0, HALF)], s["c0"].at[x, y, c], 2)
    local("c1", cot_h.at[:, pl.ds(HALF, HALF)], s["c1"].at[x, y, c], 3)
    local("x", x_h, s["xv"], 4)
    local("w", w_h, s["wv"], 5)

    def at_z(d):
        return (lax.rem(z + d, NZ), x, t)

    def at_xc(dx, dc):
        xd = lax.rem(x + dx, NX)
        cd = c if dc == 0 else 1 - c
        return xd, cd, (z, xd, 2 * y + cd)

    def at_y(dy):
        yd = lax.rem(y + dy, NY)
        return yd, (z, x, 2 * yd + c)

    def dist(k):
        half = lax.div(k + 1, 2)
        return 8 + half * (1 - 2 * lax.rem(k, 2))

    partner = (z, x, 2 * y + 1 - c)
    y1 = y + 1 - 2 * lax.rem(y, 2)
    quads = [partner, (z, x, 2 * y1 + c), (z, x, 2 * y1 + 1 - c)]
    quad_sem = [1, 2, 3]
    rows7 = [(dx, dc) for dx in range(NX) for dc in range(2) if (dx, dc) != (0, 0)]

    barrier = pltpu.get_barrier_semaphore()

    def hello(dev):
        pl.semaphore_signal(barrier, inc=1, device_id=dev, device_id_type=MESH)

    @pl.loop(0, NZ - 1)
    def _(k):
        hello(at_z(dist(k)))

    for dx, dc in rows7:
        hello(at_xc(dx, dc)[2])
    for dy in range(1, NY):
        hello(at_y(dy)[1])
    hello(quads[2])

    counter = [0]
    sent = []

    def take(n):
        first = counter[0]
        counter[0] += n
        return first

    def copy(src, dst, dev, i):
        return pltpu.make_async_remote_copy(
            src_ref=src,
            dst_ref=dst,
            send_sem=s["ps"].at[i],
            recv_sem=s["pr"].at[i],
            device_id=dev,
            device_id_type=MESH,
        )

    def push(cps):
        for cp in cps:
            cp.start()
            sent.append(cp)
        return cps

    def arrived(cps):
        for cp in cps:
            cp.wait_recv()

    def z_copy(kind, src, dst, d):
        return pltpu.make_async_remote_copy(
            src_ref=src,
            dst_ref=dst.at[z],
            send_sem=s["zs"].at[kind, d],
            recv_sem=s["zr"].at[kind, d],
            device_id=at_z(d),
            device_id_type=MESH,
        )

    def z_send(kind, src, dst):
        @pl.loop(0, NZ - 1)
        def _(k):
            d = dist(k)
            z_copy(kind, src.at[lax.rem(z + d, NZ)], dst, d).start()

    def z_wait(kind, src, dst):
        @pl.loop(0, NZ - 1)
        def _(k):
            z_copy(kind, src.at[0], dst, dist(k)).wait_recv()

    def slot_of(b):
        return slot[ten[b]]

    locals_["au"].wait()

    @pl.loop(0, NZ)
    def _(zd):
        row = slot_of(zd * BLOCKS + own_block)
        lanes = pl.ds(pl.multiple_of(quarter * QUARTER, QUARTER), QUARTER)
        s["bsend"][zd] = s["au"][row, :, lanes]

    locals_["ad"].wait()
    lane = lax.broadcasted_iota(I32, (1, RANKS), 1)
    lane2 = lax.broadcasted_iota(I32, (1, NZ * DOWN), 1)

    def gather(zd, carry):
        b_lo, b_hi = carry
        tg = jnp.zeros((1, RANKS), I32)
        for b in range(BLOCKS):
            row = slot_of(zd * BLOCKS + b)
            s["asend"][zd, b] = s["ad"][row]
            tg = jnp.where(lax.div(lane, DOWN) == b, row * DOWN + lax.rem(lane, DOWN), tg)
            here = lax.div(lane2, UP) == zd * UP + b % 4
            mine = lax.rem(lane2, UP) * SLOTS + row
            if b < 4:
                b_lo = jnp.where(here, mine, b_lo)
            else:
                b_hi = jnp.where(here, mine, b_hi)
        s["tga"][zd] = tg
        return b_lo, b_hi

    zero2 = jnp.zeros((1, NZ * DOWN), I32)
    tgb_lo, tgb_hi = lax.fori_loop(0, NZ, gather, (zero2, zero2))
    s["tgb"][0] = tgb_lo
    s["tgb"][1] = tgb_hi
    locals_["c0"].wait()
    locals_["c1"].wait()
    locals_["x"].wait()
    locals_["w"].wait()
    pl.semaphore_wait(barrier, NZ - 1 + 7 + 3 + 1)

    z_send(0, s["bsend"], s["brecv"])
    z_send(1, s["asend"], s["arecv"])
    i0 = take(2)
    pair = push(
        [
            copy(s["xv"].at[:, :, 1 - c], s["xp"], partner, i0),
            copy(s["wv"], s["wp"], partner, i0 + 1),
        ]
    )
    c0, c1 = s["c0"], s["c1"]
    i0 = take(6)
    cot1a = push(
        [
            copy(c0.at[x, y, c], c0.at[x, y, c], at_xc(d, 0)[2], i0 + d - 1)
            for d in range(1, NX)
        ]
    )
    cot1b = push(
        [
            copy(c1.at[x, y, c], c1.at[x, y, c], at_y(d)[1], i0 + 2 + d)
            for d in range(1, NY)
        ]
    )
    s["brecv"][z] = s["bsend"][z]
    s["arecv"][z] = s["asend"][z]

    arrived(pair)
    x_own = s["xv"].at[:, :, c][...].reshape(NX * NY * ROWS, FEATS)
    x_other = s["xp"][...].reshape(NX * NY * ROWS, FEATS)

    def project(j):
        cols = slice(j * QUARTER, (j + 1) * QUARTER)
        v = jnp.dot(x_own, s["wv"][:, cols], preferred_element_type=F32)
        v = v + jnp.dot(x_other, s["wp"][:, cols], preferred_element_type=F32)
        v = v.astype(BF16).reshape(NX, NY, ROWS, QUARTER)
        if j < 2:
            s["pa"][:, :, :, cols] = v
        else:
            cols = slice((j - 2) * QUARTER, (j - 1) * QUARTER)
            for xx in range(NX):
                s["pb"][:, xx, :, cols] = v[xx]

    project(0)
    project(1)
    i0 = take(3)
    rs1a = push(
        [
            copy(s["pa"].at[at_xc(d, 0)[0]], s["ra1"].at[d - 1], at_xc(d, 0)[2], i0 + d - 1)
            for d in range(1, NX)
        ]
    )
    project(2)
    project(3)

    z_wait(0, s["bsend"], s["brecv"])
    for k in range(NZ):
        s["bqf"][k * UP : (k + 1) * UP, :] = s["brecv"][k].astype(F32)
    s["bown"][quarter] = s["bqf"][...].astype(BF16)
    i0 = take(3)
    quad = push(
        [
            copy(s["bown"].at[quarter], s["bown"].at[quarter], dev, i0 + n - 1)
            for n, dev in zip(quad_sem, quads, strict=True)
        ]
    )
    arrived(quad)
    last = (((1,), (1,)), ((), ()))

    def back(ref, first):
        v = ref[x, y, c]
        a = lax.dot_general(v[:, :QUARTER], s["bown"][first], last, preferred_element_type=F32)
        b = lax.dot_general(v[:, QUARTER:], s["bown"][first + 1], last, preferred_element_type=F32)
        return a + b

    lg, la = s["lg"], s["la"]
    lg[x, y, c] = jnp.concatenate([back(c0, 0), back(c1, 2)], axis=1).astype(BF16)

    def gather_y(ref):
        i0 = take(3)
        return push(
            [
                copy(ref.at[x, y, c], ref.at[x, y, c], at_y(d)[1], i0 + d - 1)
                for d in range(1, NY)
            ]
        )

    def gather_x(ref):
        i0 = take(7)
        return push(
            [
                copy(ref.at[x, :, c], ref.at[x, :, c], at_xc(dx, dc)[2], i0 + n)
                for n, (dx, dc) in enumerate(rows7)
            ]
        )

    lgy = gather_y(lg)
    arrived(cot1a)
    i0 = take(3)
    cot2a = push(
        [
            copy(c0.at[:, y, c], c0.at[:, y, c], at_y(d)[1], i0 + d - 1)
            for d in range(1, NY)
        ]
    )
    i0 = take(3)
    rs1b = push(
        [
            copy(s["pb"].at[at_y(d)[0]], s["rb1"].at[d - 1], at_y(d)[1], i0 + d - 1)
            for d in range(1, NY)
        ]
    )
    arrived(lgy)
    lgx = gather_x(lg)
    arrived(cot1b)
    i0 = take(3)
    cot2b = push(
        [
            copy(c1.at[x, :, c], c1.at[x, :, c], at_xc(d, 0)[2], i0 + d - 1)
            for d in range(1, NX)
        ]
    )
    i3 = take(8)
    cot3 = push(
        [
            copy(c0.at[:, y, c], c0.at[:, y, c], partner, i3),
            copy(c1.at[x, :, c], c1.at[x, :, c], partner, i3 + 4),
        ]
    )

    def tok(b):
        return s["xv"][lax.div(b, 2), pl.ds(2 * lax.rem(b, 2), 2)].reshape(4 * ROWS, FEATS)

    def low_of(ref, b):
        return ref[lax.div(b, 2), pl.ds(2 * lax.rem(b, 2), 2)].reshape(4 * ROWS, RANKS)

    def down_of(b):
        return s["arecv"][:, b].reshape(FEATS, RANKS)

    first = (((0,), (0,)), ((), ()))
    arrived(lgx)

    @pl.loop(0, BLOCKS)
    def _(b):
        v = lax.dot_general(tok(b), low_of(lg, b), first, preferred_element_type=F32)
        s["gasend"][:, b] = v.astype(BF16).reshape(NZ, DOWN, RANKS)

    z_send(2, s["gasend"], s["garecv"])
    s["garecv"][z] = s["gasend"][z]

    z_wait(1, s["asend"], s["arecv"])
    lp = s["lp"]

    @pl.loop(0, BLOCKS)
    def _(b):
        v = jnp.dot(tok(b), down_of(b), preferred_element_type=F32)
        lp[lax.div(b, 2), pl.ds(2 * lax.rem(b, 2), 2)] = v.astype(BF16).reshape(2, 2, ROWS, RANKS)

    i0 = take(7)
    lowx = push(
        [
            copy(
                lp.at[at_xc(dx, dc)[0], :, at_xc(dx, dc)[1]],
                s["lr"].at[n],
                at_xc(dx, dc)[2],
                i0 + n,
            )
            for n, (dx, dc) in enumerate(rows7)
        ]
    )

    def total(own, ref, n):
        v = own.astype(F32)
        for k in range(n):
            v = v + ref[k].astype(F32)
        return v

    arrived(rs1a)
    for yy in range(NY):
        v = total(s["pa"][x, yy], s["ra1"].at[:, yy], 3)
        s["qa"][yy] = v.astype(BF16)
    arrived(lowx)
    s["lq"][...] = total(lp.at[x, :, c][...], s["lr"], 7).astype(BF16)
    i0 = take(3)
    lowy = push(
        [
            copy(s["lq"].at[at_y(d)[0]], s["ls"].at[d - 1], at_y(d)[1], i0 + d - 1)
            for d in range(1, NY)
        ]
    )
    i0 = take(3)
    rs2a = push(
        [
            copy(s["qa"].at[at_y(d)[0]], s["ra2"].at[d - 1], at_y(d)[1], i0 + d - 1)
            for d in range(1, NY)
        ]
    )
    arrived(lowy)
    low_rows = total(s["lq"][y], s["ls"], 3).astype(BF16)
    la[x, y, c] = low_rows
    lay = gather_y(la)
    for d in range(1, NY):
        cot2a[d - 1].wait_recv()
        src = lax.rem(y - d + NY, NY)
        cot3 += push([copy(c0.at[:, src, c], c0.at[:, src, c], partner, i3 + d)])
    arrived(lay)
    lax_ = gather_x(la)
    for d in range(1, NX):
        cot2b[d - 1].wait_recv()
        src = lax.rem(x - d + NX, NX)
        cot3 += push([copy(c1.at[src, :, c], c1.at[src, :, c], partner, i3 + 4 + d)])
    arrived(rs1b)
    for xx in range(NX):
        v = total(s["pb"][y, xx], s["rb1"].at[:, xx], 3)
        s["qb"][xx] = v.astype(BF16)
    i0 = take(3)
    rs2b = push(
        [
            copy(s["qb"].at[at_xc(d, 0)[0]], s["rb2"].at[d - 1], at_xc(d, 0)[2], i0 + d - 1)
            for d in range(1, NX)
        ]
    )
    arrived(lax_)
    arrived(cot3)

    group = x * 8 + t
    chunk = pl.ds(pl.multiple_of(lax.rem(lax.div(group, 2), 8) * 128, 128), 128)
    values = lax.div(group, 16)

    def cot_cols(b):
        at = (lax.div(b, 2), pl.ds(2 * lax.rem(b, 2), 2), slice(None), slice(None), chunk)
        v = jnp.where(values == 0, c0[at].astype(F32), c1[at].astype(F32))
        return v.astype(BF16).reshape(4 * ROWS, 128)

    wide = lax.broadcasted_iota(I32, (COLS, 128), 1)

    def up_part(b):
        v = lax.dot_general(low_of(la, b), cot_cols(b), first, preferred_element_type=F32)
        v = jnp.where(values == 0, v[:COLS], v[COLS:])
        return v, pltpu.roll(v, COLS, 1)

    for b4 in range(4):
        lo, lo_r = up_part(b4)
        hi, hi_r = up_part(b4 + 4)
        left = jnp.where(c == 0, lo, lo_r)
        right = jnp.where(c == 0, hi_r, hi)
        v = jnp.where(wide < COLS, left, right)
        for k in range(NZ):
            s["gbf"][k, b4 * UP : (b4 + 1) * UP, :] = v[k * UP : (k + 1) * UP]
    s["gbsend"][...] = s["gbf"][...].astype(BF16)
    z_send(3, s["gbsend"], s["gbrecv"])
    s["gbrecv"][z] = s["gbsend"][z]

    @pl.loop(0, NX)
    def _(xx):
        rows = NY * 2 * ROWS
        v = lax.dot_general(
            c0[xx].reshape(rows, HALF), s["wv"][:, :HALF], last, preferred_element_type=F32
        )
        v = v + lax.dot_general(
            c1[xx].reshape(rows, HALF), s["wv"][:, HALF:], last, preferred_element_type=F32
        )
        low = [
            lax.dot_general(low_of(lg, 2 * xx + k), down_of(2 * xx + k), last, preferred_element_type=F32)
            for k in range(2)
        ]
        s["igv"][xx] = (v + jnp.concatenate(low, axis=0)).astype(BF16)

    local("ig", s["igv"], ig_o, 6)

    arrived(rs2a)
    arrived(rs2b)
    low_rows = la[x, y, c]
    for j in range(4):
        cols = slice((j % 2) * QUARTER, (j % 2 + 1) * QUARTER)
        if j < 2:
            own, r1, r2 = s["pa"][x, y, :, cols], s["ra1"].at[:, y, :, cols], s["ra2"].at[:, :, cols]
        else:
            own, r1, r2 = s["pb"][y, x, :, cols], s["rb1"].at[:, x, :, cols], s["rb2"].at[:, :, cols]
        side = low_rows[:, :COLS] if j < 2 else low_rows[:, COLS:]
        v = total(total(own, r1, 3), r2, 3)
        v = v + jnp.dot(side, s["bown"][j], preferred_element_type=F32)
        s["kvv"][:, j * QUARTER : (j + 1) * QUARTER] = v.astype(BF16)
    local("kv", s["kvv"], kv_o, 7)

    def pick(ref, kind, dst, ks):
        for k in ks:
            z_copy(kind, ref.at[0], dst, k).wait_recv()

    order = [0] + [8 + ((k + 1) // 2) * (1 - 2 * (k % 2)) for k in range(NZ - 1)]
    high = 128
    for part in range(4):
        ds = order[4 * part : 4 * part + 4]
        pick(s["gasend"], 2, s["garecv"], [d for d in ds if d])
        srcs = [lax.rem(z - d + NZ, NZ) for d in ds]
        tg = jnp.concatenate([s["tga"][k] for k in srcs], axis=1)
        data = jnp.concatenate([s["garecv"][k].reshape(BLOCKS * DOWN, RANKS) for k in srcs], axis=0)

        @pl.loop(0, SLOTS * DOWN // high)
        def _(r, part=part, tg=tg, data=data):
            at = pl.ds(pl.multiple_of(r * high, high), high)
            ids = lax.broadcasted_iota(I32, (high, 4 * RANKS), 0) + r * high
            sel = jnp.where(ids == tg, 1.0, 0.0).astype(BF16)
            v = jnp.dot(sel, data, preferred_element_type=F32)
            if part:
                v = v + s["gaacc"][at, :]
            s["gaacc"][at, :] = v

    local("ga", s["gaacc"], ga_o, 8)
    z_wait(3, s["gbsend"], s["gbrecv"])
    data = s["gbrecv"][...].reshape(NZ * DOWN, RANKS)
    ids = lax.broadcasted_iota(I32, (UP * SLOTS, NZ * DOWN), 0)
    sums = []
    for h in range(2):
        sel = jnp.where(ids == s["tgb"][h], 1.0, 0.0).astype(BF16)
        sums.append(jnp.dot(sel, data, preferred_element_type=F32))
    for i in range(UP):
        at = slice(i * SLOTS, (i + 1) * SLOTS)
        lo, hi = sums[0][at].T, sums[1][at].T
        s["gbt"][i] = lo[:COLS] + hi[COLS:]
    local("gb", s["gbt"], gb_o, 9)

    for cp in sent:
        cp.wait_send()

    @pl.loop(1, NZ)
    def _(d):
        z_copy(0, s["bsend"].at[0], s["brecv"], d).wait_send()
        z_copy(1, s["asend"].at[0], s["arecv"], d).wait_send()
        z_copy(2, s["gasend"].at[0], s["garecv"], d).wait_send()
        z_copy(3, s["gbsend"].at[0], s["gbrecv"], d).wait_send()

    for name in ("ig", "kv", "ga", "gb"):
        locals_[name].wait()


def body(tokens, weight, down, up, tenant_of_block, slot_of_tenant, cotangent):
    sc = scratches()
    anywhere = pl.BlockSpec(memory_space=pl.ANY)
    scalars = pl.BlockSpec(memory_space=pltpu.SMEM)
    kv, ig, ga, gb = pl.pallas_call(
        functools.partial(kern, tuple(sc)),
        out_shape=(
            jax.ShapeDtypeStruct((ROWS, WIDTH), BF16),
            jax.ShapeDtypeStruct((NX, NY * 2 * ROWS, FEATS), BF16),
            jax.ShapeDtypeStruct((SLOTS * DOWN, RANKS), F32),
            jax.ShapeDtypeStruct((UP, COLS, SLOTS), F32),
        ),
        in_specs=[scalars] * 2 + [anywhere] * 5,
        out_specs=(anywhere,) * 4,
        scratch_shapes=list(sc.values()),
        compiler_params=pltpu.CompilerParams(
            collective_id=0, has_side_effects=True, vmem_limit_bytes=60 * 1024 * 1024
        ),
    )(
        tenant_of_block,
        slot_of_tenant,
        tokens.reshape(NX, NY, 2, ROWS, FEATS),
        weight,
        down,
        up,
        cotangent,
    )
    return (
        kv,
        ig.reshape(NX * NY * 2 * ROWS, FEATS),
        ga.reshape(SLOTS, DOWN, RANKS),
        gb.transpose(2, 0, 1),
    )


def solution(mesh):
    placed = (
        P("dp", ("pipe", "tensor")),
        P(("pipe", "tensor"), None),
        P(None, ("pipe", "tensor", "dp"), None),
        P(None, "dp", None),
        P(),
        P(),
        P(("dp", "pipe", "tensor"), None),
    )
    return jax.shard_map(
        body,
        mesh=mesh,
        in_specs=placed,
        out_specs=(
            P(("dp", "pipe", "tensor"), None),
            P("dp", ("pipe", "tensor")),
            P(None, ("pipe", "tensor", "dp"), None),
            P(None, "dp", ("pipe", "tensor")),
        ),
        check_vma=False,
    )
```

```python
import functools

import jax
import jax.numpy as jnp
from jax import lax
from jax.experimental import pallas as pl
from jax.experimental.pallas import tpu as pltpu
from jax.sharding import PartitionSpec as P

MESH = pl.DeviceIdType.MESH
F32, BF16, I32 = jnp.float32, jnp.bfloat16, jnp.int32
NZ, NX, NY = 16, 4, 4
SLOTS, UP, DOWN, RANKS = 96, 4, 16, 128
BLOCKS = 8
ROWS, FEATS, WIDTH, HALF, QUARTER = 32, 256, 2048, 1024, 512
COLS = 64
GROUPS = 29


def scratches():
    return dict(
        au=pltpu.VMEM((SLOTS, UP, WIDTH), BF16),
        ad=pltpu.VMEM((SLOTS, DOWN, RANKS), BF16),
        xv=pltpu.VMEM((NX, NY, 2, ROWS, FEATS), BF16),
        wv=pltpu.VMEM((FEATS, WIDTH), BF16),
        xp=pltpu.VMEM((NX, NY, ROWS, FEATS), BF16),
        wp=pltpu.VMEM((FEATS, WIDTH), BF16),
        bsend=pltpu.VMEM((NZ, UP, QUARTER), BF16),
        brecv=pltpu.VMEM((NZ, UP, QUARTER), BF16),
        bqf=pltpu.VMEM((NZ * UP, QUARTER), F32),
        bown=pltpu.VMEM((4, NZ * UP, QUARTER), BF16),
        asend=pltpu.VMEM((NZ, BLOCKS, DOWN, RANKS), BF16),
        arecv=pltpu.VMEM((NZ, BLOCKS, DOWN, RANKS), BF16),
        c0=pltpu.VMEM((NX, NY, 2, ROWS, HALF), BF16),
        c1=pltpu.VMEM((NX, NY, 2, ROWS, HALF), BF16),
        pa=pltpu.VMEM((NX, NY, ROWS, HALF), BF16),
        pb=pltpu.VMEM((NY, NX, ROWS, HALF), BF16),
        ra1=pltpu.VMEM((3, NY, ROWS, HALF), BF16),
        rb1=pltpu.VMEM((3, NX, ROWS, HALF), BF16),
        qa=pltpu.VMEM((NY, ROWS, HALF), BF16),
        qb=pltpu.VMEM((NX, ROWS, HALF), BF16),
        ra2=pltpu.VMEM((3, ROWS, HALF), BF16),
        rb2=pltpu.VMEM((3, ROWS, HALF), BF16),
        cq=pltpu.VMEM((4, ROWS, QUARTER), BF16),
        phs=pltpu.VMEM((COLS, RANKS), F32),
        phr=pltpu.VMEM((COLS, RANKS), F32),
        lgp=pltpu.VMEM((NX, NY, COLS, RANKS), BF16),
        lgm=pltpu.VMEM((BLOCKS, 4 * ROWS, RANKS), BF16),
        lp=pltpu.VMEM((NX, NY, 2, ROWS, RANKS), BF16),
        lr=pltpu.VMEM((7, NY, ROWS, RANKS), BF16),
        lq=pltpu.VMEM((NY, ROWS, RANKS), BF16),
        ls=pltpu.VMEM((3, ROWS, RANKS), BF16),
        la=pltpu.VMEM((NX, NY, 2, ROWS, RANKS), BF16),
        gaf=pltpu.VMEM((FEATS * BLOCKS, RANKS), F32),
        gasend=pltpu.VMEM((NZ, BLOCKS, DOWN * RANKS), BF16),
        garecv=pltpu.VMEM((NZ, BLOCKS, DOWN * RANKS), BF16),
        gbf=pltpu.VMEM((NZ, DOWN, RANKS), F32),
        gbsend=pltpu.VMEM((NZ, DOWN, RANKS), BF16),
        gbrecv=pltpu.VMEM((NZ, DOWN, RANKS), BF16),
        tga=pltpu.VMEM((1, NZ * BLOCKS), I32),
        tgb=pltpu.VMEM((2, 1, NZ * DOWN), I32),
        ten=pltpu.SMEM((NZ * BLOCKS,), I32),
        slot=pltpu.SMEM((SLOTS,), I32),
        loc=pltpu.SemaphoreType.DMA((13,)),
        zs=pltpu.SemaphoreType.DMA((4,)),
        zr=pltpu.SemaphoreType.DMA((4,)),
        ps=pltpu.SemaphoreType.DMA((GROUPS,)),
        pr=pltpu.SemaphoreType.DMA((GROUPS,)),
    )


def kern(names, ten_h, slot_h, x_h, w_h, ad_h, au_h, cot_h, kv_o, ig_o, ga_o, gb_o, *refs):
    s = dict(zip(names, refs, strict=True))
    z, x, t = lax.axis_index("dp"), lax.axis_index("pipe"), lax.axis_index("tensor")
    y, c = lax.div(t, 2), lax.rem(t, 2)
    own_block = x * 2 + lax.div(y, 2)
    quarter = lax.rem(t, 4)

    locals_ = {}

    def quarter_lanes(q):
        return pl.ds(pl.multiple_of(q * QUARTER, QUARTER), QUARTER)

    def local(name, src, dst, i):
        cp = pltpu.make_async_copy(src, dst, s["loc"].at[i])
        cp.start()
        locals_[name] = cp

    def at_z(d):
        return (lax.rem(z + d, NZ), x, t)

    def at_xc(dx, dc):
        xd = lax.rem(x + dx, NX)
        cd = c if dc == 0 else 1 - c
        return xd, cd, (z, xd, 2 * y + cd)

    def at_y(dy):
        yd = lax.rem(y + dy, NY)
        return yd, (z, x, 2 * yd + c)

    def dist(k):
        half = lax.div(k + 1, 2)
        return 8 + half * (1 - 2 * lax.rem(k, 2))

    partner = (z, x, 2 * y + 1 - c)
    y1 = y + 1 - 2 * lax.rem(y, 2)
    quad_of = [quarter + 1 - 2 * c, lax.rem(quarter + 2, 4), lax.rem(quarter + 3 - 2 * c, 4)]
    quads = [partner, (z, x, 2 * y1 + c), (z, x, 2 * y1 + 1 - c)]
    rows7 = [(dx, dc) for dx in range(NX) for dc in range(2) if (dx, dc) != (0, 0)]

    barrier = pltpu.get_barrier_semaphore()

    def hello(dev):
        pl.semaphore_signal(barrier, inc=1, device_id=dev, device_id_type=MESH)

    @pl.loop(0, NZ - 1)
    def _(k):
        hello(at_z(dist(k)))

    for dx, dc in rows7:
        hello(at_xc(dx, dc)[2])
    for dy in range(1, NY):
        hello(at_y(dy)[1])
    hello(quads[2])
    local("ten", ten_h, s["ten"], 10)
    local("slot", slot_h, s["slot"], 11)
    local("au", au_h, s["au"], 0)
    local("ad", ad_h, s["ad"], 1)
    local("c0", cot_h.at[:, pl.ds(0, HALF)], s["c0"].at[x, y, c], 2)
    local("c1", cot_h.at[:, pl.ds(HALF, HALF)], s["c1"].at[x, y, c], 3)
    local("cq", cot_h.at[:, quarter_lanes(quarter)], s["cq"].at[quarter], 9)
    local("x", x_h, s["xv"], 4)
    local("w", w_h, s["wv"], 5)

    groups = []

    def until(ref, sem):
        pltpu.make_async_copy(ref, ref, sem).wait()

    def push(like, *copies):
        i = len(groups)
        groups.append(like)
        for src, dst, dev in copies:
            pltpu.make_async_remote_copy(
                src_ref=src,
                dst_ref=dst,
                send_sem=s["ps"].at[i],
                recv_sem=s["pr"].at[i],
                device_id=dev,
                device_id_type=MESH,
            ).start()
        return i

    def arrived(*ids):
        for i in ids:
            until(groups[i], s["pr"].at[i])

    def z_send(kind, src, dst, lo=0, hi=NZ - 1):
        @pl.loop(lo, hi)
        def _(k):
            d = dist(k)
            pltpu.make_async_remote_copy(
                src_ref=src.at[lax.rem(z + d, NZ)],
                dst_ref=dst.at[z],
                send_sem=s["zs"].at[kind],
                recv_sem=s["zr"].at[kind],
                device_id=at_z(d),
                device_id_type=MESH,
            ).start()

    def z_wait(kind, ref):
        until(ref.at[pl.ds(0, NZ - 1)], s["zr"].at[kind])

    def slot_of(b):
        return s["slot"][s["ten"][b]]

    locals_["ten"].wait()
    locals_["slot"].wait()
    locals_["au"].wait()

    @pl.loop(0, NZ)
    def _(zd):
        row = slot_of(zd * BLOCKS + own_block)
        s["bsend"][zd] = s["au"][row, :, quarter_lanes(quarter)]

    locals_["ad"].wait()
    lane = lax.broadcasted_iota(I32, (1, RANKS), 1)
    lane2 = lax.broadcasted_iota(I32, (1, NZ * DOWN), 1)

    def gather(zd, carry):
        slots, b_lo, b_hi = carry
        for b in range(BLOCKS):
            row = slot_of(zd * BLOCKS + b)
            s["asend"][zd, b] = s["ad"][row]
            slots = jnp.where(lane == zd * BLOCKS + b, row, slots)
            here = lax.div(lane2, UP) == zd * UP + b % 4
            mine = lax.rem(lane2, UP) * SLOTS + row
            if b < 4:
                b_lo = jnp.where(here, mine, b_lo)
            else:
                b_hi = jnp.where(here, mine, b_hi)
        return slots, b_lo, b_hi

    zero2 = jnp.zeros((1, NZ * DOWN), I32)
    zero1 = jnp.zeros((1, NZ * BLOCKS), I32)
    s["tga"][...], s["tgb"][0], s["tgb"][1] = lax.fori_loop(0, NZ, gather, (zero1, zero2, zero2))
    locals_["c0"].wait()
    locals_["c1"].wait()
    locals_["x"].wait()
    locals_["w"].wait()
    pl.semaphore_wait(barrier, NZ - 1 + 7 + 3 + 1)

    c0, c1, lgp, la, lp = s["c0"], s["c1"], s["lgp"], s["la"], s["lp"]
    piece = s["ra1"]
    z_send(0, s["bsend"], s["brecv"])
    z_send(1, s["asend"], s["arecv"])
    pair = [
        push(s["xp"], (s["xv"].at[:, :, 1 - c], s["xp"], partner)),
        push(s["wp"], (s["wv"], s["wp"], partner)),
    ]
    own0, own1 = c0.at[x, y, c], c1.at[x, y, c]
    cot1 = [
        push(s["ra2"], *[(own0, own0, at_xc(d, 0)[2]) for d in (1, 3, 2)]),
        push(s["rb2"], *[(own1, own1, at_y(d)[1]) for d in (1, 3, 2)]),
    ]
    quad_rows = push(
        s["cq"].at[pl.ds(0, 3)],
        *[
            (cot_h.at[:, quarter_lanes(q)], s["cq"].at[quarter], dev)
            for q, dev in zip(quad_of, quads, strict=True)
        ],
    )
    s["brecv"][z] = s["bsend"][z]
    s["arecv"][z] = s["asend"][z]

    arrived(*pair)
    x_own = s["xv"].at[:, :, c][...].reshape(NX * NY * ROWS, FEATS)
    x_other = s["xp"][...].reshape(NX * NY * ROWS, FEATS)

    def project(j):
        cols = slice(j * QUARTER, (j + 1) * QUARTER)
        v = jnp.dot(x_own, s["wv"][:, cols], preferred_element_type=F32)
        v = v + jnp.dot(x_other, s["wp"][:, cols], preferred_element_type=F32)
        v = v.astype(BF16).reshape(NX, NY, ROWS, QUARTER)
        if j < 2:
            s["pa"][:, :, :, cols] = v
        else:
            cols = slice((j - 2) * QUARTER, (j - 1) * QUARTER)
            for xx in range(NX):
                s["pb"][:, xx, :, cols] = v[xx]

    for j in range(4):
        project(j)

    two = piece.at[pl.ds(0, 2)]

    def scatter_y(ds):
        return [(s["pb"].at[at_y(d)[0]], s["rb1"].at[d - 1], at_y(d)[1]) for d in ds]

    def scatter_y2(h):
        rows = pl.ds(2 * h, 2)
        yd, dev = at_y(2)
        return (s["pb"].at[yd, rows], s["rb1"].at[1, rows], dev)

    def scatter_x(ds):
        return [(s["pa"].at[at_xc(d, 0)[0]], s["ra1"].at[d - 1], at_xc(d, 0)[2]) for d in ds]

    rs1a = [push(two, *scatter_x((1, 3)))]
    rs1b = [push(two, *scatter_y((1, 3)))]
    mine0, mine1 = c0.at[:, y, c], c1.at[x, :, c]
    cot2a, cot2b, cot3 = [], [], []

    def to_partner(n, ref, where, ds):
        at = [ref.at[where(d)] for d in ds]
        cot3.append(push(piece.at[pl.ds(0, n)] if n > 1 else piece.at[0], *[(r, r, partner) for r in at]))

    def col(d):
        return (slice(None), lax.rem(y - d + NY, NY), c)

    def row(d):
        return (lax.rem(x - d + NX, NX), slice(None), c)

    arrived(*cot1)
    cot2b.append(push(two, *[(mine1, mine1, at_xc(d, 0)[2]) for d in (1, 3)]))
    cot3.append(push(two, (mine0, mine0, partner), (mine1, mine1, partner)))
    z_wait(0, s["bsend"])
    for k in range(NZ):
        s["bqf"][k * UP : (k + 1) * UP, :] = s["brecv"][k].astype(F32)
    up_own = s["bqf"][...].astype(BF16)
    s["bown"][quarter] = up_own
    last = (((1,), (1,)), ((), ()))
    arrived(quad_rows)
    locals_["cq"].wait()
    v = lax.dot_general(
        s["cq"][...].reshape(4 * ROWS, QUARTER), up_own, last, preferred_element_type=F32
    )
    v = jnp.concatenate([v[:COLS], v[COLS:]], axis=1)
    s["phs"][...] = v
    arrived(push(s["phr"], (s["phs"], s["phr"], partner)))
    lgp[x, y] = (v + s["phr"][...]).astype(BF16)
    mine = lgp.at[x, y]
    lgy = push(lgp.at[0, pl.ds(0, 3)], *[(mine, mine, at_y(d)[1]) for d in (1, 3, 2)])
    part = s["bown"].at[quarter]
    quad = push(s["bown"].at[pl.ds(0, 3)], *[(part, part, dev) for dev in quads])
    cot2a.append(push(two, *[(mine0, mine0, at_y(d)[1]) for d in (1, 3)]))
    cot2a.append(push(piece.at[0], (mine0, mine0, at_y(2)[1])))

    def gather_y(ref):
        r = ref.at[x, y, c]
        return push(s["ls"], *[(r, r, at_y(d)[1]) for d in (1, 3, 2)])

    def gather_x(ref):
        r = ref.at[x, :, c]
        return push(s["lr"], *[(r, r, at_xc(dx, dc)[2]) for dx, dc in rows7])

    arrived(lgy)
    mine = lgp.at[x]
    lgx = push(lgp.at[pl.ds(0, 3)], *[(mine, mine, at_xc(d, 0)[2]) for d in (1, 3, 2)])
    cot2b.append(push(piece.at[0], (mine1, mine1, at_xc(2, 0)[2])))

    def tok(b):
        return s["xv"][b // 2, 2 * (b % 2) : 2 * (b % 2) + 2].reshape(4 * ROWS, FEATS)

    def low_of(ref, b):
        return ref[b // 2, 2 * (b % 2) : 2 * (b % 2) + 2].reshape(4 * ROWS, RANKS)

    def down_of(b):
        return s["arecv"][:, b].reshape(FEATS, RANKS)

    first = (((0,), (0,)), ((), ()))
    arrived(lgx)
    narrow = lax.broadcasted_iota(I32, (COLS, RANKS), 1) < COLS
    for b in range(BLOCKS):
        key = lgp[b // 2, 2 * (b % 2)].astype(F32)
        val = lgp[b // 2, 2 * (b % 2) + 1].astype(F32)
        top = jnp.where(narrow, key, pltpu.roll(val, COLS, 1))
        bottom = jnp.where(narrow, pltpu.roll(key, COLS, 1), val)
        v = jnp.concatenate([top, bottom], axis=0).astype(BF16)
        s["lgm"][b] = v
        v = lax.dot_general(tok(b), v, first, preferred_element_type=F32)
        s["gaf"][pl.ds(b, FEATS, stride=BLOCKS), :] = v

    @pl.loop(0, NZ)
    def _(k):
        for r in range(DOWN):
            at = pl.ds(pl.multiple_of((k * DOWN + r) * BLOCKS, BLOCKS), BLOCKS)
            s["gasend"][k, :, r * RANKS : (r + 1) * RANKS] = s["gaf"][at, :].astype(BF16)

    z_send(2, s["gasend"], s["garecv"], 9, 15)
    s["garecv"][z] = s["gasend"][z]

    arrived(cot2a[0], cot2b[0])
    to_partner(2, c0, col, (1, 3))
    to_partner(2, c1, row, (1, 3))

    z_wait(1, s["asend"])

    for b in range(BLOCKS):
        v = jnp.dot(tok(b), down_of(b), preferred_element_type=F32)
        lp[b // 2, 2 * (b % 2) : 2 * (b % 2) + 2] = v.astype(BF16).reshape(2, 2, ROWS, RANKS)

    lowx = push(
        s["lr"],
        *[
            (lp.at[at_xc(dx, dc)[0], :, at_xc(dx, dc)[1]], s["lr"].at[n], at_xc(dx, dc)[2])
            for n, (dx, dc) in enumerate(rows7)
        ],
    )
    z_send(2, s["gasend"], s["garecv"], 0, 9)
    half = piece.at[0, pl.ds(0, 2)]
    rs1b.append(push(half, scatter_y2(0)))

    arrived(cot2b[1], cot2a[1])
    to_partner(1, c1, row, (2,))
    to_partner(1, c0, col, (2,))

    def total(own, ref, n):
        v = own.astype(F32)
        for k in range(n):
            v = v + ref[k].astype(F32)
        return v

    arrived(lowx)
    s["lq"][...] = total(lp.at[x, :, c][...], s["lr"], 7).astype(BF16)
    lowy = push(
        s["ls"], *[(s["lq"].at[at_y(d)[0]], s["ls"].at[d - 1], at_y(d)[1]) for d in (1, 3, 2)]
    )
    rs1a.append(push(piece.at[0], *scatter_x((2,))))

    arrived(*cot3)

    for xx in range(NX):
        rows = NY * 2 * ROWS
        v = lax.dot_general(
            c0[xx].reshape(rows, HALF), s["wv"][:, :HALF], last, preferred_element_type=F32
        )
        v = v + lax.dot_general(
            c1[xx].reshape(rows, HALF), s["wv"][:, HALF:], last, preferred_element_type=F32
        )
        low = [
            lax.dot_general(s["lgm"][2 * xx + k], down_of(2 * xx + k), last, preferred_element_type=F32)
            for k in range(2)
        ]
        ig_o[xx] = (v + jnp.concatenate(low, axis=0)).astype(BF16)


    arrived(lowy)
    la[x, y, c] = total(s["lq"][y], s["ls"], 3).astype(BF16)
    lay = gather_y(la)
    arrived(lay)
    last_low = gather_x(la)
    rs1b.append(push(half, scatter_y2(1)))
    arrived(*rs1a)
    for yy in range(NY):
        v = total(s["pa"][x, yy], s["ra1"].at[:, yy], 3)
        s["qa"][yy] = v.astype(BF16)
    rs2a = push(
        s["ra2"], *[(s["qa"].at[at_y(d)[0]], s["ra2"].at[d - 1], at_y(d)[1]) for d in (1, 3, 2)]
    )
    arrived(last_low)

    group = x * 8 + t
    chunk = pl.ds(pl.multiple_of(lax.rem(lax.div(group, 2), 8) * 128, 128), 128)
    values = lax.div(group, 16)

    def cot_cols(b):
        at = (b // 2, slice(2 * (b % 2), 2 * (b % 2) + 2), slice(None), slice(None), chunk)
        v = jnp.where(values == 0, c0[at].astype(F32), c1[at].astype(F32))
        return v.astype(BF16).reshape(4 * ROWS, 128)

    wide = lax.broadcasted_iota(I32, (COLS, 128), 1)

    def up_part(b):
        v = lax.dot_general(low_of(la, b), cot_cols(b), first, preferred_element_type=F32)
        v = jnp.where(values == 0, v[:COLS], v[COLS:])
        return v, pltpu.roll(v, COLS, 1)

    for b4 in range(4):
        lo, lo_r = up_part(b4)
        hi, hi_r = up_part(b4 + 4)
        left = jnp.where(c == 0, lo, lo_r)
        right = jnp.where(c == 0, hi_r, hi)
        v = jnp.where(wide < COLS, left, right)
        for k in range(NZ):
            s["gbf"][k, b4 * UP : (b4 + 1) * UP, :] = v[k * UP : (k + 1) * UP]
    s["gbsend"][...] = s["gbf"][...].astype(BF16)
    z_send(3, s["gbsend"], s["gbrecv"])
    s["gbrecv"][z] = s["gbsend"][z]

    arrived(*rs1b)
    for xx in range(NX):
        v = total(s["pb"][y, xx], s["rb1"].at[:, xx], 3)
        s["qb"][xx] = v.astype(BF16)
    rs2b = push(
        s["rb2"],
        *[(s["qb"].at[at_xc(d, 0)[0]], s["rb2"].at[d - 1], at_xc(d, 0)[2]) for d in (1, 3, 2)],
    )
    arrived(rs2a, rs2b, quad)
    low_rows = la[x, y, c]
    for j in range(4):
        cols = slice((j % 2) * QUARTER, (j % 2 + 1) * QUARTER)
        if j < 2:
            own, r1, r2 = s["pa"][x, y, :, cols], s["ra1"].at[:, y, :, cols], s["ra2"].at[:, :, cols]
        else:
            own, r1, r2 = s["pb"][y, x, :, cols], s["rb1"].at[:, x, :, cols], s["rb2"].at[:, :, cols]
        side = low_rows[:, :COLS] if j < 2 else low_rows[:, COLS:]
        v = total(total(own, r1, 3), r2, 3)
        v = v + jnp.dot(side, s["bown"][j], preferred_element_type=F32)
        kv_o[:, j * QUARTER : (j + 1) * QUARTER] = v.astype(BF16)

    ids = lax.broadcasted_iota(I32, (SLOTS, NZ * BLOCKS), 0)
    sel = jnp.where(ids == s["tga"][...], 1.0, 0.0).astype(BF16)
    z_wait(2, s["gasend"])
    for r in range(DOWN):
        lanes = slice(r * RANKS, (r + 1) * RANKS)
        data = s["garecv"][:, :, lanes].astype(F32).reshape(NZ * BLOCKS, RANKS).astype(BF16)
        v = jnp.dot(sel, data, preferred_element_type=F32)
        ga_o[pl.ds(r, SLOTS, stride=DOWN), :] = v

    z_wait(3, s["gbsend"])
    data = s["gbrecv"][...].reshape(NZ * DOWN, RANKS)
    ids = lax.broadcasted_iota(I32, (UP * SLOTS, NZ * DOWN), 0)
    sums = []
    for h in range(2):
        sel = jnp.where(ids == s["tgb"][h], 1.0, 0.0).astype(BF16)
        sums.append(jnp.dot(sel, data, preferred_element_type=F32))
    for i in range(UP):
        at = slice(i * SLOTS, (i + 1) * SLOTS)
        lo, hi = sums[0][at].T, sums[1][at].T
        gb_o[i] = lo[:COLS] + hi[COLS:]

    for i, like in enumerate(groups):
        until(like, s["ps"].at[i])
    for kind, name in enumerate(("bsend", "asend", "gasend", "gbsend")):
        until(s[name].at[pl.ds(0, NZ - 1)], s["zs"].at[kind])
    assert len(groups) == GROUPS, len(groups)

def body(tokens, weight, down, up, tenant_of_block, slot_of_tenant, cotangent):
    sc = scratches()
    anywhere = pl.BlockSpec(memory_space=pl.ANY)
    vmem = pl.BlockSpec(memory_space=pltpu.VMEM)
    results = (
        ((ROWS, WIDTH), BF16),
        ((NX, NY * 2 * ROWS, FEATS), BF16),
        ((SLOTS * DOWN, RANKS), F32),
        ((UP, COLS, SLOTS), F32),
    )
    kv, ig, ga, gb = pl.pallas_call(
        functools.partial(kern, tuple(sc)),
        out_shape=tuple(pltpu.VMEM(shape, kind) for shape, kind in results),
        in_specs=[anywhere] * 7,
        out_specs=(vmem,) * 4,
        scratch_shapes=list(sc.values()),
        compiler_params=pltpu.CompilerParams(
            collective_id=0, has_side_effects=True, vmem_limit_bytes=60 * 1024 * 1024
        ),
    )(
        tenant_of_block,
        slot_of_tenant,
        tokens.reshape(NX, NY, 2, ROWS, FEATS),
        weight,
        down,
        up,
        cotangent,
    )
    return (
        kv,
        ig.reshape(NX * NY * 2 * ROWS, FEATS),
        ga.reshape(SLOTS, DOWN, RANKS),
        gb.transpose(2, 0, 1),
    )


def solution(mesh):
    placed = (
        P("dp", ("pipe", "tensor")),
        P(("pipe", "tensor"), None),
        P(None, ("pipe", "tensor", "dp"), None),
        P(None, "dp", None),
        P(),
        P(),
        P(("dp", "pipe", "tensor"), None),
    )
    return jax.shard_map(
        body,
        mesh=mesh,
        in_specs=placed,
        out_specs=(
            P(("dp", "pipe", "tensor"), None),
            P("dp", ("pipe", "tensor")),
            P(None, ("pipe", "tensor", "dp"), None),
            P(None, "dp", ("pipe", "tensor")),
        ),
        check_vma=False,
    )
```

```python
import functools

import jax
import jax.numpy as jnp
from jax import lax
from jax.experimental import pallas as pl
from jax.experimental.pallas import tpu as pltpu
from jax.sharding import PartitionSpec as P

MESH = pl.DeviceIdType.MESH
F32, BF16, I32 = jnp.float32, jnp.bfloat16, jnp.int32
NZ, NX, NY = 16, 4, 4
SLOTS, UP, DOWN, RANKS = 96, 4, 16, 128
BLOCKS = 8
ROWS, FEATS, WIDTH, HALF, QUARTER = 32, 256, 2048, 1024, 512
COLS = 64
GROUPS = 28


def scratches():
    return dict(
        au=pltpu.VMEM((SLOTS, UP, WIDTH), BF16),
        ad=pltpu.VMEM((SLOTS, DOWN, RANKS), BF16),
        xv=pltpu.VMEM((NX, NY, 2, ROWS, FEATS), BF16),
        wv=pltpu.VMEM((FEATS, WIDTH), BF16),
        xp=pltpu.VMEM((NX, NY, ROWS, FEATS), BF16),
        wp=pltpu.VMEM((FEATS, WIDTH), BF16),
        bsend=pltpu.VMEM((NZ, UP, QUARTER), BF16),
        brecv=pltpu.VMEM((NZ, UP, QUARTER), BF16),
        bqf=pltpu.VMEM((NZ * UP, QUARTER), F32),
        bown=pltpu.VMEM((4, NZ * UP, QUARTER), BF16),
        asend=pltpu.VMEM((NZ, BLOCKS, DOWN, RANKS), BF16),
        arecv=pltpu.VMEM((NZ, BLOCKS, DOWN, RANKS), BF16),
        c0=pltpu.VMEM((NX, NY, 2, ROWS, HALF), BF16),
        c1=pltpu.VMEM((NX, NY, 2, ROWS, HALF), BF16),
        pa=pltpu.VMEM((NX, NY, ROWS, HALF), BF16),
        pb=pltpu.VMEM((NY, NX, ROWS, HALF), BF16),
        ra1=pltpu.VMEM((3, NY, ROWS, HALF), BF16),
        rb1=pltpu.VMEM((3, NX, ROWS, HALF), BF16),
        qa=pltpu.VMEM((NY, ROWS, HALF), BF16),
        qb=pltpu.VMEM((NX, ROWS, HALF), BF16),
        ra2=pltpu.VMEM((3, ROWS, HALF), BF16),
        rb2=pltpu.VMEM((3, ROWS, HALF), BF16),
        cq=pltpu.VMEM((4, ROWS, QUARTER), BF16),
        phs=pltpu.VMEM((COLS, RANKS), F32),
        phr=pltpu.VMEM((COLS, RANKS), F32),
        lgp=pltpu.VMEM((NX, NY, COLS, RANKS), BF16),
        lgm=pltpu.VMEM((BLOCKS, 4 * ROWS, RANKS), BF16),
        lp=pltpu.VMEM((NX, NY, 2, ROWS, RANKS), BF16),
        lr=pltpu.VMEM((7, NY, ROWS, RANKS), BF16),
        lq=pltpu.VMEM((NY, ROWS, RANKS), BF16),
        ls=pltpu.VMEM((3, ROWS, RANKS), BF16),
        la=pltpu.VMEM((NX, NY, 2, ROWS, RANKS), BF16),
        gaf=pltpu.VMEM((FEATS * BLOCKS, RANKS), F32),
        gasend=pltpu.VMEM((NZ, BLOCKS, DOWN * RANKS), BF16),
        garecv=pltpu.VMEM((NZ, BLOCKS, DOWN * RANKS), BF16),
        gbf=pltpu.VMEM((NZ, DOWN, RANKS), F32),
        gbsend=pltpu.VMEM((NZ, DOWN, RANKS), BF16),
        gbrecv=pltpu.VMEM((NZ, DOWN, RANKS), BF16),
        tga=pltpu.VMEM((1, NZ * BLOCKS), I32),
        tgb=pltpu.VMEM((2, 1, NZ * DOWN), I32),
        ten=pltpu.SMEM((NZ * BLOCKS,), I32),
        slot=pltpu.SMEM((SLOTS,), I32),
        loc=pltpu.SemaphoreType.DMA((13,)),
        zs=pltpu.SemaphoreType.DMA((4,)),
        zr=pltpu.SemaphoreType.DMA((4,)),
        ps=pltpu.SemaphoreType.DMA((GROUPS,)),
        pr=pltpu.SemaphoreType.DMA((GROUPS,)),
    )


def kern(names, ten_h, slot_h, x_h, w_h, ad_h, au_h, cot_h, kv_o, ig_o, ga_o, gb_o, *refs):
    s = dict(zip(names, refs, strict=True))
    z, x, t = lax.axis_index("dp"), lax.axis_index("pipe"), lax.axis_index("tensor")
    y, c = lax.div(t, 2), lax.rem(t, 2)
    own_block = x * 2 + lax.div(y, 2)
    quarter = lax.rem(t, 4)

    locals_ = {}

    def quarter_lanes(q):
        return pl.ds(pl.multiple_of(q * QUARTER, QUARTER), QUARTER)

    def local(name, src, dst, i):
        cp = pltpu.make_async_copy(src, dst, s["loc"].at[i])
        cp.start()
        locals_[name] = cp

    def at_z(d):
        return (lax.rem(z + d, NZ), x, t)

    def at_xc(dx, dc):
        xd = lax.rem(x + dx, NX)
        cd = c if dc == 0 else 1 - c
        return xd, cd, (z, xd, 2 * y + cd)

    def at_y(dy):
        yd = lax.rem(y + dy, NY)
        return yd, (z, x, 2 * yd + c)

    def dist(k):
        half = lax.div(k + 1, 2)
        return 8 + half * (1 - 2 * lax.rem(k, 2))

    partner = (z, x, 2 * y + 1 - c)
    y1 = y + 1 - 2 * lax.rem(y, 2)
    quad_of = [quarter + 1 - 2 * c, lax.rem(quarter + 2, 4), lax.rem(quarter + 3 - 2 * c, 4)]
    quads = [partner, (z, x, 2 * y1 + c), (z, x, 2 * y1 + 1 - c)]
    rows7 = [(dx, dc) for dx in range(NX) for dc in range(2) if (dx, dc) != (0, 0)]

    barrier = pltpu.get_barrier_semaphore()

    def hello(dev):
        pl.semaphore_signal(barrier, inc=1, device_id=dev, device_id_type=MESH)

    @pl.loop(0, NZ - 1)
    def _(k):
        hello(at_z(dist(k)))

    for dx, dc in rows7:
        hello(at_xc(dx, dc)[2])
    for dy in range(1, NY):
        hello(at_y(dy)[1])
    hello(quads[2])
    local("ten", ten_h, s["ten"], 10)
    local("slot", slot_h, s["slot"], 11)
    local("au", au_h, s["au"], 0)
    local("ad", ad_h, s["ad"], 1)
    local("c0", cot_h.at[:, pl.ds(0, HALF)], s["c0"].at[x, y, c], 2)
    local("c1", cot_h.at[:, pl.ds(HALF, HALF)], s["c1"].at[x, y, c], 3)
    local("cq", cot_h.at[:, quarter_lanes(quarter)], s["cq"].at[quarter], 9)
    local("x", x_h, s["xv"], 4)
    local("w", w_h, s["wv"], 5)

    groups = []

    def until(ref, sem):
        pltpu.make_async_copy(ref, ref, sem).wait()

    def push(like, *copies):
        i = len(groups)
        groups.append(like)
        for src, dst, dev in copies:
            pltpu.make_async_remote_copy(
                src_ref=src,
                dst_ref=dst,
                send_sem=s["ps"].at[i],
                recv_sem=s["pr"].at[i],
                device_id=dev,
                device_id_type=MESH,
            ).start()
        return i

    def arrived(*ids):
        for i in ids:
            until(groups[i], s["pr"].at[i])

    def z_send(kind, src, dst, lo=0, hi=NZ - 1):
        @pl.loop(lo, hi)
        def _(k):
            d = dist(k)
            pltpu.make_async_remote_copy(
                src_ref=src.at[lax.rem(z + d, NZ)],
                dst_ref=dst.at[z],
                send_sem=s["zs"].at[kind],
                recv_sem=s["zr"].at[kind],
                device_id=at_z(d),
                device_id_type=MESH,
            ).start()

    def z_wait(kind, ref):
        until(ref.at[pl.ds(0, NZ - 1)], s["zr"].at[kind])

    def slot_of(b):
        return s["slot"][s["ten"][b]]

    locals_["ten"].wait()
    locals_["slot"].wait()
    locals_["au"].wait()

    @pl.loop(0, NZ)
    def _(zd):
        row = slot_of(zd * BLOCKS + own_block)
        s["bsend"][zd] = s["au"][row, :, quarter_lanes(quarter)]

    locals_["ad"].wait()
    lane = lax.broadcasted_iota(I32, (1, RANKS), 1)
    lane2 = lax.broadcasted_iota(I32, (1, NZ * DOWN), 1)

    def gather(zd, carry):
        slots, b_lo, b_hi = carry
        for b in range(BLOCKS):
            row = slot_of(zd * BLOCKS + b)
            s["asend"][zd, b] = s["ad"][row]
            slots = jnp.where(lane == zd * BLOCKS + b, row, slots)
            here = lax.div(lane2, UP) == zd * UP + b % 4
            mine = lax.rem(lane2, UP) * SLOTS + row
            if b < 4:
                b_lo = jnp.where(here, mine, b_lo)
            else:
                b_hi = jnp.where(here, mine, b_hi)
        return slots, b_lo, b_hi

    zero2 = jnp.zeros((1, NZ * DOWN), I32)
    zero1 = jnp.zeros((1, NZ * BLOCKS), I32)
    s["tga"][...], s["tgb"][0], s["tgb"][1] = lax.fori_loop(0, NZ, gather, (zero1, zero2, zero2))
    locals_["c0"].wait()
    locals_["c1"].wait()
    locals_["x"].wait()
    locals_["w"].wait()
    pl.semaphore_wait(barrier, NZ - 1 + 7 + 3 + 1)

    c0, c1, lgp, la, lp = s["c0"], s["c1"], s["lgp"], s["la"], s["lp"]
    piece = s["ra1"]
    z_send(0, s["bsend"], s["brecv"])
    z_send(1, s["asend"], s["arecv"])
    pair = [
        push(s["xp"], (s["xv"].at[:, :, 1 - c], s["xp"], partner)),
        push(s["wp"], (s["wv"], s["wp"], partner)),
    ]
    own0, own1 = c0.at[x, y, c], c1.at[x, y, c]
    cot1 = [
        push(s["ra2"], *[(own0, own0, at_xc(d, 0)[2]) for d in (1, 3, 2)]),
        push(s["rb2"], *[(own1, own1, at_y(d)[1]) for d in (1, 3, 2)]),
    ]
    quad_rows = push(
        s["cq"].at[pl.ds(0, 3)],
        *[
            (cot_h.at[:, quarter_lanes(q)], s["cq"].at[quarter], dev)
            for q, dev in zip(quad_of, quads, strict=True)
        ],
    )
    s["brecv"][z] = s["bsend"][z]
    s["arecv"][z] = s["asend"][z]

    arrived(*pair)
    x_own = s["xv"].at[:, :, c][...].reshape(NX * NY * ROWS, FEATS)
    x_other = s["xp"][...].reshape(NX * NY * ROWS, FEATS)

    def project(j):
        cols = slice(j * QUARTER, (j + 1) * QUARTER)
        v = jnp.dot(x_own, s["wv"][:, cols], preferred_element_type=F32)
        v = v + jnp.dot(x_other, s["wp"][:, cols], preferred_element_type=F32)
        v = v.astype(BF16).reshape(NX, NY, ROWS, QUARTER)
        if j < 2:
            s["pa"][:, :, :, cols] = v
        else:
            cols = slice((j - 2) * QUARTER, (j - 1) * QUARTER)
            for xx in range(NX):
                s["pb"][:, xx, :, cols] = v[xx]

    for j in range(4):
        project(j)

    two = piece.at[pl.ds(0, 2)]

    def scatter_y(ds):
        return [(s["pb"].at[at_y(d)[0]], s["rb1"].at[d - 1], at_y(d)[1]) for d in ds]

    def scatter_x(ds):
        return [(s["pa"].at[at_xc(d, 0)[0]], s["ra1"].at[d - 1], at_xc(d, 0)[2]) for d in ds]

    rs1a = [push(two, *scatter_x((1, 3)))]
    rs1b = [push(two, *scatter_y((1, 3)))]
    mine0, mine1 = c0.at[:, y, c], c1.at[x, :, c]
    cot2a, cot2b, cot3 = [], [], []

    def to_partner(n, ref, where, ds):
        at = [ref.at[where(d)] for d in ds]
        cot3.append(push(piece.at[pl.ds(0, n)] if n > 1 else piece.at[0], *[(r, r, partner) for r in at]))

    def col(d):
        return (slice(None), lax.rem(y - d + NY, NY), c)

    def row(d):
        return (lax.rem(x - d + NX, NX), slice(None), c)

    arrived(*cot1)
    cot2b.append(push(two, *[(mine1, mine1, at_xc(d, 0)[2]) for d in (1, 3)]))
    cot3.append(push(two, (mine0, mine0, partner), (mine1, mine1, partner)))
    z_wait(0, s["bsend"])
    for k in range(NZ):
        s["bqf"][k * UP : (k + 1) * UP, :] = s["brecv"][k].astype(F32)
    up_own = s["bqf"][...].astype(BF16)
    s["bown"][quarter] = up_own
    last = (((1,), (1,)), ((), ()))
    arrived(quad_rows)
    locals_["cq"].wait()
    v = lax.dot_general(
        s["cq"][...].reshape(4 * ROWS, QUARTER), up_own, last, preferred_element_type=F32
    )
    v = jnp.concatenate([v[:COLS], v[COLS:]], axis=1)
    s["phs"][...] = v
    arrived(push(s["phr"], (s["phs"], s["phr"], partner)))
    lgp[x, y] = (v + s["phr"][...]).astype(BF16)
    mine = lgp.at[x, y]
    lgy = push(lgp.at[0, pl.ds(0, 3)], *[(mine, mine, at_y(d)[1]) for d in (1, 3, 2)])

    def gather_y(ref):
        r = ref.at[x, y, c]
        return push(s["ls"], *[(r, r, at_y(d)[1]) for d in (1, 3, 2)])

    def gather_x(ref):
        r = ref.at[x, :, c]
        return push(s["lr"], *[(r, r, at_xc(dx, dc)[2]) for dx, dc in rows7])

    cot2a.append(push(two, *[(mine0, mine0, at_y(d)[1]) for d in (1, 3)]))
    cot2a.append(push(piece.at[0], (mine0, mine0, at_y(2)[1])))
    arrived(lgy)
    mine = lgp.at[x]
    lgx = push(lgp.at[pl.ds(0, 3)], *[(mine, mine, at_xc(d, 0)[2]) for d in (1, 3, 2)])
    cot2b.append(push(piece.at[0], (mine1, mine1, at_xc(2, 0)[2])))
    part = s["bown"].at[quarter]
    quad = push(s["bown"].at[pl.ds(0, 3)], *[(part, part, dev) for dev in quads])

    def tok(b):
        return s["xv"][b // 2, 2 * (b % 2) : 2 * (b % 2) + 2].reshape(4 * ROWS, FEATS)

    def low_of(ref, b):
        return ref[b // 2, 2 * (b % 2) : 2 * (b % 2) + 2].reshape(4 * ROWS, RANKS)

    def down_of(b):
        return s["arecv"][:, b].reshape(FEATS, RANKS)

    first = (((0,), (0,)), ((), ()))
    arrived(lgx)
    narrow = lax.broadcasted_iota(I32, (COLS, RANKS), 1) < COLS
    for b in range(BLOCKS):
        key = lgp[b // 2, 2 * (b % 2)].astype(F32)
        val = lgp[b // 2, 2 * (b % 2) + 1].astype(F32)
        top = jnp.where(narrow, key, pltpu.roll(val, COLS, 1))
        bottom = jnp.where(narrow, pltpu.roll(key, COLS, 1), val)
        v = jnp.concatenate([top, bottom], axis=0).astype(BF16)
        s["lgm"][b] = v
        v = lax.dot_general(tok(b), v, first, preferred_element_type=F32)
        s["gaf"][pl.ds(b, FEATS, stride=BLOCKS), :] = v

    @pl.loop(0, NZ)
    def _(k):
        for r in range(DOWN):
            at = pl.ds(pl.multiple_of((k * DOWN + r) * BLOCKS, BLOCKS), BLOCKS)
            s["gasend"][k, :, r * RANKS : (r + 1) * RANKS] = s["gaf"][at, :].astype(BF16)

    z_send(2, s["gasend"], s["garecv"], 9, 13)
    s["garecv"][z] = s["gasend"][z]

    arrived(cot2a[0], cot2b[0])
    to_partner(2, c0, col, (1, 3))
    to_partner(2, c1, row, (1, 3))

    z_wait(1, s["asend"])

    for b in range(BLOCKS):
        v = jnp.dot(tok(b), down_of(b), preferred_element_type=F32)
        lp[b // 2, 2 * (b % 2) : 2 * (b % 2) + 2] = v.astype(BF16).reshape(2, 2, ROWS, RANKS)

    lowx = push(
        s["lr"],
        *[
            (lp.at[at_xc(dx, dc)[0], :, at_xc(dx, dc)[1]], s["lr"].at[n], at_xc(dx, dc)[2])
            for n, (dx, dc) in enumerate(rows7)
        ],
    )
    z_send(2, s["gasend"], s["garecv"], 0, 9)
    rs1b.append(push(piece.at[0], *scatter_y((2,))))

    arrived(cot2b[1], cot2a[1])
    to_partner(1, c1, row, (2,))
    to_partner(1, c0, col, (2,))

    def total(own, ref, n):
        v = own.astype(F32)
        for k in range(n):
            v = v + ref[k].astype(F32)
        return v

    arrived(lowx)
    s["lq"][...] = total(lp.at[x, :, c][...], s["lr"], 7).astype(BF16)
    lowy = push(
        s["ls"], *[(s["lq"].at[at_y(d)[0]], s["ls"].at[d - 1], at_y(d)[1]) for d in (1, 3, 2)]
    )
    rs1a.append(push(piece.at[0], *scatter_x((2,))))

    arrived(*cot3)

    for xx in range(NX):
        rows = NY * 2 * ROWS
        v = lax.dot_general(
            c0[xx].reshape(rows, HALF), s["wv"][:, :HALF], last, preferred_element_type=F32
        )
        v = v + lax.dot_general(
            c1[xx].reshape(rows, HALF), s["wv"][:, HALF:], last, preferred_element_type=F32
        )
        low = [
            lax.dot_general(s["lgm"][2 * xx + k], down_of(2 * xx + k), last, preferred_element_type=F32)
            for k in range(2)
        ]
        ig_o[xx] = (v + jnp.concatenate(low, axis=0)).astype(BF16)


    arrived(lowy)
    la[x, y, c] = total(s["lq"][y], s["ls"], 3).astype(BF16)
    lay = gather_y(la)
    arrived(lay)
    last_low = gather_x(la)
    arrived(*rs1a)
    for yy in range(NY):
        v = total(s["pa"][x, yy], s["ra1"].at[:, yy], 3)
        s["qa"][yy] = v.astype(BF16)
    rs2a = push(
        s["ra2"], *[(s["qa"].at[at_y(d)[0]], s["ra2"].at[d - 1], at_y(d)[1]) for d in (1, 3, 2)]
    )
    arrived(last_low)

    group = x * 8 + t
    chunk = pl.ds(pl.multiple_of(lax.rem(lax.div(group, 2), 8) * 128, 128), 128)
    values = lax.div(group, 16)

    def cot_cols(b):
        at = (b // 2, slice(2 * (b % 2), 2 * (b % 2) + 2), slice(None), slice(None), chunk)
        v = jnp.where(values == 0, c0[at].astype(F32), c1[at].astype(F32))
        return v.astype(BF16).reshape(4 * ROWS, 128)

    wide = lax.broadcasted_iota(I32, (COLS, 128), 1)

    def up_part(b):
        v = lax.dot_general(low_of(la, b), cot_cols(b), first, preferred_element_type=F32)
        v = jnp.where(values == 0, v[:COLS], v[COLS:])
        return v, pltpu.roll(v, COLS, 1)

    for b4 in range(4):
        lo, lo_r = up_part(b4)
        hi, hi_r = up_part(b4 + 4)
        left = jnp.where(c == 0, lo, lo_r)
        right = jnp.where(c == 0, hi_r, hi)
        v = jnp.where(wide < COLS, left, right)
        for k in range(NZ):
            s["gbf"][k, b4 * UP : (b4 + 1) * UP, :] = v[k * UP : (k + 1) * UP]
    s["gbsend"][...] = s["gbf"][...].astype(BF16)
    z_send(3, s["gbsend"], s["gbrecv"])
    z_send(2, s["gasend"], s["garecv"], 13, 15)
    s["gbrecv"][z] = s["gbsend"][z]

    arrived(*rs1b)
    for xx in range(NX):
        v = total(s["pb"][y, xx], s["rb1"].at[:, xx], 3)
        s["qb"][xx] = v.astype(BF16)
    rs2b = push(
        s["rb2"],
        *[(s["qb"].at[at_xc(d, 0)[0]], s["rb2"].at[d - 1], at_xc(d, 0)[2]) for d in (1, 3, 2)],
    )

    ids = lax.broadcasted_iota(I32, (SLOTS, NZ * BLOCKS), 0)
    sel = jnp.where(ids == s["tga"][...], 1.0, 0.0).astype(BF16)
    z_wait(2, s["gasend"])
    for r in range(DOWN):
        lanes = slice(r * RANKS, (r + 1) * RANKS)
        data = s["garecv"][:, :, lanes].astype(F32).reshape(NZ * BLOCKS, RANKS).astype(BF16)
        v = jnp.dot(sel, data, preferred_element_type=F32)
        ga_o[pl.ds(r, SLOTS, stride=DOWN), :] = v

    arrived(rs2a, rs2b, quad)
    low_rows = la[x, y, c]
    for j in range(4):
        cols = slice((j % 2) * QUARTER, (j % 2 + 1) * QUARTER)
        if j < 2:
            own, r1, r2 = s["pa"][x, y, :, cols], s["ra1"].at[:, y, :, cols], s["ra2"].at[:, :, cols]
        else:
            own, r1, r2 = s["pb"][y, x, :, cols], s["rb1"].at[:, x, :, cols], s["rb2"].at[:, :, cols]
        side = low_rows[:, :COLS] if j < 2 else low_rows[:, COLS:]
        v = total(total(own, r1, 3), r2, 3)
        v = v + jnp.dot(side, s["bown"][j], preferred_element_type=F32)
        kv_o[:, j * QUARTER : (j + 1) * QUARTER] = v.astype(BF16)

    z_wait(3, s["gbsend"])
    data = s["gbrecv"][...].reshape(NZ * DOWN, RANKS)
    ids = lax.broadcasted_iota(I32, (UP * SLOTS, NZ * DOWN), 0)
    sums = []
    for h in range(2):
        sel = jnp.where(ids == s["tgb"][h], 1.0, 0.0).astype(BF16)
        sums.append(jnp.dot(sel, data, preferred_element_type=F32))
    for i in range(UP):
        at = slice(i * SLOTS, (i + 1) * SLOTS)
        lo, hi = sums[0][at].T, sums[1][at].T
        gb_o[i] = lo[:COLS] + hi[COLS:]

    for i, like in enumerate(groups):
        until(like, s["ps"].at[i])
    for kind, name in enumerate(("bsend", "asend", "gasend", "gbsend")):
        until(s[name].at[pl.ds(0, NZ - 1)], s["zs"].at[kind])
    assert len(groups) == GROUPS, len(groups)

def write_out(kv, ig, ga, gb, kv_o, ig_o, ga_o, gb_o, sem):
    pairs = ((ga, ga_o), (ig, ig_o), (kv, kv_o), (gb, gb_o))
    copies = [pltpu.make_async_copy(v, o, sem.at[i]) for i, (v, o) in enumerate(pairs)]
    for cp in copies:
        cp.start()
    for cp in copies:
        cp.wait()


def body(tokens, weight, down, up, tenant_of_block, slot_of_tenant, cotangent):
    sc = scratches()
    anywhere = pl.BlockSpec(memory_space=pl.ANY)
    vmem = pl.BlockSpec(memory_space=pltpu.VMEM)
    results = (
        ((ROWS, WIDTH), BF16),
        ((NX, NY * 2 * ROWS, FEATS), BF16),
        ((SLOTS * DOWN, RANKS), F32),
        ((UP, COLS, SLOTS), F32),
    )
    kv, ig, ga, gb = pl.pallas_call(
        functools.partial(kern, tuple(sc)),
        out_shape=tuple(pltpu.VMEM(shape, kind) for shape, kind in results),
        in_specs=[anywhere] * 7,
        out_specs=(vmem,) * 4,
        scratch_shapes=list(sc.values()),
        compiler_params=pltpu.CompilerParams(
            collective_id=0, has_side_effects=True, vmem_limit_bytes=60 * 1024 * 1024
        ),
    )(
        tenant_of_block,
        slot_of_tenant,
        tokens.reshape(NX, NY, 2, ROWS, FEATS),
        weight,
        down,
        up,
        cotangent,
    )
    near = [pltpu.with_memory_space_constraint(v, pltpu.VMEM) for v in (kv, ig, ga, gb)]
    kv, ig, ga, gb = pl.pallas_call(
        write_out,
        out_shape=tuple(jax.ShapeDtypeStruct(shape, kind) for shape, kind in results),
        in_specs=[vmem] * 4,
        out_specs=(anywhere,) * 4,
        scratch_shapes=[pltpu.SemaphoreType.DMA((4,))],
    )(*near)
    return (
        kv,
        ig.reshape(NX * NY * 2 * ROWS, FEATS),
        ga.reshape(SLOTS, DOWN, RANKS),
        gb.transpose(2, 0, 1),
    )


def solution(mesh):
    placed = (
        P("dp", ("pipe", "tensor")),
        P(("pipe", "tensor"), None),
        P(None, ("pipe", "tensor", "dp"), None),
        P(None, "dp", None),
        P(),
        P(),
        P(("dp", "pipe", "tensor"), None),
    )
    return jax.shard_map(
        body,
        mesh=mesh,
        in_specs=placed,
        out_specs=(
            P(("dp", "pipe", "tensor"), None),
            P("dp", ("pipe", "tensor")),
            P(None, ("pipe", "tensor", "dp"), None),
            P(None, "dp", ("pipe", "tensor")),
        ),
        check_vma=False,
    )
```

```python
import functools

import jax
import jax.numpy as jnp
from jax import lax
from jax.experimental import pallas as pl
from jax.experimental.pallas import tpu as pltpu
from jax.sharding import PartitionSpec as P

MESH = pl.DeviceIdType.MESH
F32, BF16, I32 = jnp.float32, jnp.bfloat16, jnp.int32
NZ, NX, NY = 16, 4, 4
SLOTS, UP, DOWN, RANKS = 96, 4, 16, 128
BLOCKS = 8
ROWS, FEATS, WIDTH, HALF, QUARTER = 32, 256, 2048, 1024, 512
COLS = 64
GROUPS = 28


def scratches():
    return dict(
        au=pltpu.VMEM((SLOTS, UP, WIDTH), BF16),
        ad=pltpu.VMEM((SLOTS, DOWN, RANKS), BF16),
        xv=pltpu.VMEM((NX, NY, 2, ROWS, FEATS), BF16),
        wv=pltpu.VMEM((FEATS, WIDTH), BF16),
        xp=pltpu.VMEM((NX, NY, ROWS, FEATS), BF16),
        wp=pltpu.VMEM((FEATS, WIDTH), BF16),
        bsend=pltpu.VMEM((NZ, UP, QUARTER), BF16),
        brecv=pltpu.VMEM((NZ, UP, QUARTER), BF16),
        bqf=pltpu.VMEM((NZ * UP, QUARTER), F32),
        bown=pltpu.VMEM((4, NZ * UP, QUARTER), BF16),
        asend=pltpu.VMEM((NZ, BLOCKS, DOWN, RANKS), BF16),
        arecv=pltpu.VMEM((NZ, BLOCKS, DOWN, RANKS), BF16),
        c0=pltpu.VMEM((NX, NY, 2, ROWS, HALF), BF16),
        c1=pltpu.VMEM((NX, NY, 2, ROWS, HALF), BF16),
        pa=pltpu.VMEM((NX, NY, ROWS, HALF), BF16),
        pb=pltpu.VMEM((NY, NX, ROWS, HALF), BF16),
        ra1=pltpu.VMEM((3, NY, ROWS, HALF), BF16),
        rb1=pltpu.VMEM((3, NX, ROWS, HALF), BF16),
        qa=pltpu.VMEM((NY, ROWS, HALF), BF16),
        qb=pltpu.VMEM((NX, ROWS, HALF), BF16),
        ra2=pltpu.VMEM((3, ROWS, HALF), BF16),
        rb2=pltpu.VMEM((3, ROWS, HALF), BF16),
        cq=pltpu.VMEM((4, ROWS, QUARTER), BF16),
        phs=pltpu.VMEM((COLS, RANKS), F32),
        phr=pltpu.VMEM((COLS, RANKS), F32),
        lgp=pltpu.VMEM((NX, NY, COLS, RANKS), BF16),
        lgm=pltpu.VMEM((BLOCKS, 4 * ROWS, RANKS), BF16),
        lp=pltpu.VMEM((NX, NY, 2, ROWS, RANKS), BF16),
        lr=pltpu.VMEM((7, NY, ROWS, RANKS), BF16),
        lq=pltpu.VMEM((NY, ROWS, RANKS), BF16),
        ls=pltpu.VMEM((3, ROWS, RANKS), BF16),
        la=pltpu.VMEM((NX, NY, 2, ROWS, RANKS), BF16),
        gaf=pltpu.VMEM((FEATS * BLOCKS, RANKS), F32),
        gasend=pltpu.VMEM((NZ, BLOCKS, DOWN * RANKS), BF16),
        garecv=pltpu.VMEM((NZ, BLOCKS, DOWN * RANKS), BF16),
        gbf=pltpu.VMEM((NZ, DOWN, RANKS), F32),
        gbsend=pltpu.VMEM((NZ, DOWN, RANKS), BF16),
        gbrecv=pltpu.VMEM((NZ, DOWN, RANKS), BF16),
        tga=pltpu.VMEM((1, NZ * BLOCKS), I32),
        tgb=pltpu.VMEM((2, 1, NZ * DOWN), I32),
        ten=pltpu.SMEM((NZ * BLOCKS,), I32),
        slot=pltpu.SMEM((SLOTS,), I32),
        loc=pltpu.SemaphoreType.DMA((13,)),
        zs=pltpu.SemaphoreType.DMA((4,)),
        zr=pltpu.SemaphoreType.DMA((4,)),
        ps=pltpu.SemaphoreType.DMA((GROUPS,)),
        pr=pltpu.SemaphoreType.DMA((GROUPS,)),
    )


def kern(names, ten_h, slot_h, x_h, w_h, ad_h, au_h, cot_h, kv_o, ig_o, ga_o, gb_o, *refs):
    s = dict(zip(names, refs, strict=True))
    z, x, t = lax.axis_index("dp"), lax.axis_index("pipe"), lax.axis_index("tensor")
    y, c = lax.div(t, 2), lax.rem(t, 2)
    own_block = x * 2 + lax.div(y, 2)
    quarter = lax.rem(t, 4)

    locals_ = {}

    def quarter_lanes(q):
        return pl.ds(pl.multiple_of(q * QUARTER, QUARTER), QUARTER)

    def local(name, src, dst, i):
        cp = pltpu.make_async_copy(src, dst, s["loc"].at[i])
        cp.start()
        locals_[name] = cp

    def at_z(d):
        return (lax.rem(z + d, NZ), x, t)

    def at_xc(dx, dc):
        xd = lax.rem(x + dx, NX)
        cd = c if dc == 0 else 1 - c
        return xd, cd, (z, xd, 2 * y + cd)

    def at_y(dy):
        yd = lax.rem(y + dy, NY)
        return yd, (z, x, 2 * yd + c)

    def dist(k):
        half = lax.div(k + 1, 2)
        return 8 + half * (1 - 2 * lax.rem(k, 2))

    partner = (z, x, 2 * y + 1 - c)
    y1 = y + 1 - 2 * lax.rem(y, 2)
    quad_of = [quarter + 1 - 2 * c, lax.rem(quarter + 2, 4), lax.rem(quarter + 3 - 2 * c, 4)]
    quads = [partner, (z, x, 2 * y1 + c), (z, x, 2 * y1 + 1 - c)]
    rows7 = [(dx, dc) for dx in range(NX) for dc in range(2) if (dx, dc) != (0, 0)]

    barrier = pltpu.get_barrier_semaphore()

    def hello(dev):
        pl.semaphore_signal(barrier, inc=1, device_id=dev, device_id_type=MESH)

    @pl.loop(0, NZ - 1)
    def _(k):
        hello(at_z(dist(k)))

    for dx, dc in rows7:
        hello(at_xc(dx, dc)[2])
    for dy in range(1, NY):
        hello(at_y(dy)[1])
    hello(quads[2])
    local("ten", ten_h, s["ten"], 10)
    local("slot", slot_h, s["slot"], 11)
    local("au", au_h, s["au"], 0)
    local("ad", ad_h, s["ad"], 1)
    local("c0", cot_h.at[:, pl.ds(0, HALF)], s["c0"].at[x, y, c], 2)
    local("c1", cot_h.at[:, pl.ds(HALF, HALF)], s["c1"].at[x, y, c], 3)
    local("cq", cot_h.at[:, quarter_lanes(quarter)], s["cq"].at[quarter], 9)
    local("x", x_h, s["xv"], 4)
    local("w", w_h, s["wv"], 5)

    groups = []

    def until(ref, sem):
        pltpu.make_async_copy(ref, ref, sem).wait()

    def push(like, *copies):
        i = len(groups)
        groups.append(like)
        for src, dst, dev in copies:
            pltpu.make_async_remote_copy(
                src_ref=src,
                dst_ref=dst,
                send_sem=s["ps"].at[i],
                recv_sem=s["pr"].at[i],
                device_id=dev,
                device_id_type=MESH,
            ).start()
        return i

    def arrived(*ids):
        for i in ids:
            until(groups[i], s["pr"].at[i])

    def z_send(kind, src, dst, lo=0, hi=NZ - 1):
        @pl.loop(lo, hi)
        def _(k):
            d = dist(k)
            pltpu.make_async_remote_copy(
                src_ref=src.at[lax.rem(z + d, NZ)],
                dst_ref=dst.at[z],
                send_sem=s["zs"].at[kind],
                recv_sem=s["zr"].at[kind],
                device_id=at_z(d),
                device_id_type=MESH,
            ).start()

    def z_wait(kind, ref):
        until(ref.at[pl.ds(0, NZ - 1)], s["zr"].at[kind])

    def slot_of(b):
        return s["slot"][s["ten"][b]]

    locals_["ten"].wait()
    locals_["slot"].wait()
    locals_["au"].wait()

    @pl.loop(0, NZ)
    def _(zd):
        row = slot_of(zd * BLOCKS + own_block)
        s["bsend"][zd] = s["au"][row, :, quarter_lanes(quarter)]

    locals_["ad"].wait()
    lane = lax.broadcasted_iota(I32, (1, RANKS), 1)
    lane2 = lax.broadcasted_iota(I32, (1, NZ * DOWN), 1)

    def gather(zd, carry):
        slots, b_lo, b_hi = carry
        for b in range(BLOCKS):
            row = slot_of(zd * BLOCKS + b)
            s["asend"][zd, b] = s["ad"][row]
            slots = jnp.where(lane == zd * BLOCKS + b, row, slots)
            here = lax.div(lane2, UP) == zd * UP + b % 4
            mine = lax.rem(lane2, UP) * SLOTS + row
            if b < 4:
                b_lo = jnp.where(here, mine, b_lo)
            else:
                b_hi = jnp.where(here, mine, b_hi)
        return slots, b_lo, b_hi

    zero2 = jnp.zeros((1, NZ * DOWN), I32)
    zero1 = jnp.zeros((1, NZ * BLOCKS), I32)
    s["tga"][...], s["tgb"][0], s["tgb"][1] = lax.fori_loop(0, NZ, gather, (zero1, zero2, zero2))
    locals_["c0"].wait()
    locals_["c1"].wait()
    locals_["x"].wait()
    locals_["w"].wait()
    pl.semaphore_wait(barrier, NZ - 1 + 7 + 3 + 1)

    c0, c1, lgp, la, lp = s["c0"], s["c1"], s["lgp"], s["la"], s["lp"]
    piece = s["ra1"]
    z_send(0, s["bsend"], s["brecv"])
    z_send(1, s["asend"], s["arecv"])
    pair = [
        push(s["xp"], (s["xv"].at[:, :, 1 - c], s["xp"], partner)),
        push(s["wp"], (s["wv"], s["wp"], partner)),
    ]
    own0, own1 = c0.at[x, y, c], c1.at[x, y, c]
    cot1 = [
        push(s["ra2"], *[(own0, own0, at_xc(d, 0)[2]) for d in (1, 3, 2)]),
        push(s["rb2"], *[(own1, own1, at_y(d)[1]) for d in (1, 3, 2)]),
    ]
    quad_rows = push(
        s["cq"].at[pl.ds(0, 3)],
        *[
            (cot_h.at[:, quarter_lanes(q)], s["cq"].at[quarter], dev)
            for q, dev in zip(quad_of, quads, strict=True)
        ],
    )
    s["brecv"][z] = s["bsend"][z]
    s["arecv"][z] = s["asend"][z]

    arrived(*pair)
    x_own = s["xv"].at[:, :, c][...].reshape(NX * NY * ROWS, FEATS)
    x_other = s["xp"][...].reshape(NX * NY * ROWS, FEATS)

    def project(j):
        cols = slice(j * QUARTER, (j + 1) * QUARTER)
        v = jnp.dot(x_own, s["wv"][:, cols], preferred_element_type=F32)
        v = v + jnp.dot(x_other, s["wp"][:, cols], preferred_element_type=F32)
        v = v.astype(BF16).reshape(NX, NY, ROWS, QUARTER)
        if j < 2:
            s["pa"][:, :, :, cols] = v
        else:
            cols = slice((j - 2) * QUARTER, (j - 1) * QUARTER)
            for xx in range(NX):
                s["pb"][:, xx, :, cols] = v[xx]

    for j in range(4):
        project(j)

    two = piece.at[pl.ds(0, 2)]

    def scatter_y(ds):
        return [(s["pb"].at[at_y(d)[0]], s["rb1"].at[d - 1], at_y(d)[1]) for d in ds]

    def scatter_x(ds):
        return [(s["pa"].at[at_xc(d, 0)[0]], s["ra1"].at[d - 1], at_xc(d, 0)[2]) for d in ds]

    rs1a = [push(two, *scatter_x((1, 3)))]
    rs1b = [push(two, *scatter_y((1, 3)))]
    mine0, mine1 = c0.at[:, y, c], c1.at[x, :, c]
    cot2a, cot2b, cot3 = [], [], []

    def to_partner(n, ref, where, ds):
        at = [ref.at[where(d)] for d in ds]
        cot3.append(push(piece.at[pl.ds(0, n)] if n > 1 else piece.at[0], *[(r, r, partner) for r in at]))

    def col(d):
        return (slice(None), lax.rem(y - d + NY, NY), c)

    def row(d):
        return (lax.rem(x - d + NX, NX), slice(None), c)

    arrived(*cot1)
    cot2b.append(push(two, *[(mine1, mine1, at_xc(d, 0)[2]) for d in (1, 3)]))
    cot3.append(push(two, (mine0, mine0, partner), (mine1, mine1, partner)))
    z_wait(0, s["bsend"])
    for k in range(NZ):
        s["bqf"][k * UP : (k + 1) * UP, :] = s["brecv"][k].astype(F32)
    up_own = s["bqf"][...].astype(BF16)
    s["bown"][quarter] = up_own
    last = (((1,), (1,)), ((), ()))
    arrived(quad_rows)
    locals_["cq"].wait()
    v = lax.dot_general(
        s["cq"][...].reshape(4 * ROWS, QUARTER), up_own, last, preferred_element_type=F32
    )
    v = jnp.concatenate([v[:COLS], v[COLS:]], axis=1)
    s["phs"][...] = v
    arrived(push(s["phr"], (s["phs"], s["phr"], partner)))
    lgp[x, y] = (v + s["phr"][...]).astype(BF16)
    mine = lgp.at[x, y]
    lgy = push(lgp.at[0, pl.ds(0, 3)], *[(mine, mine, at_y(d)[1]) for d in (1, 3, 2)])

    def gather_y(ref):
        r = ref.at[x, y, c]
        return push(s["ls"], *[(r, r, at_y(d)[1]) for d in (1, 3, 2)])

    def gather_x(ref):
        r = ref.at[x, :, c]
        return push(s["lr"], *[(r, r, at_xc(dx, dc)[2]) for dx, dc in rows7])

    cot2a.append(push(two, *[(mine0, mine0, at_y(d)[1]) for d in (1, 3)]))
    rs1b.append(push(piece.at[0], *scatter_y((2,))))
    arrived(lgy)
    mine = lgp.at[x]
    lgx = push(lgp.at[pl.ds(0, 3)], *[(mine, mine, at_xc(d, 0)[2]) for d in (1, 3, 2)])
    part = s["bown"].at[quarter]
    quad = push(s["bown"].at[pl.ds(0, 3)], *[(part, part, dev) for dev in quads])

    def tok(b):
        return s["xv"][b // 2, 2 * (b % 2) : 2 * (b % 2) + 2].reshape(4 * ROWS, FEATS)

    def low_of(ref, b):
        return ref[b // 2, 2 * (b % 2) : 2 * (b % 2) + 2].reshape(4 * ROWS, RANKS)

    def down_of(b):
        return s["arecv"][:, b].reshape(FEATS, RANKS)

    first = (((0,), (0,)), ((), ()))
    arrived(lgx)
    narrow = lax.broadcasted_iota(I32, (COLS, RANKS), 1) < COLS
    for b in range(BLOCKS):
        key = lgp[b // 2, 2 * (b % 2)].astype(F32)
        val = lgp[b // 2, 2 * (b % 2) + 1].astype(F32)
        top = jnp.where(narrow, key, pltpu.roll(val, COLS, 1))
        bottom = jnp.where(narrow, pltpu.roll(key, COLS, 1), val)
        v = jnp.concatenate([top, bottom], axis=0).astype(BF16)
        s["lgm"][b] = v
        v = lax.dot_general(tok(b), v, first, preferred_element_type=F32)
        s["gaf"][pl.ds(b, FEATS, stride=BLOCKS), :] = v

    @pl.loop(0, NZ)
    def _(k):
        for r in range(DOWN):
            at = pl.ds(pl.multiple_of((k * DOWN + r) * BLOCKS, BLOCKS), BLOCKS)
            s["gasend"][k, :, r * RANKS : (r + 1) * RANKS] = s["gaf"][at, :].astype(BF16)

    z_send(2, s["gasend"], s["garecv"], 9, 13)
    s["garecv"][z] = s["gasend"][z]

    arrived(cot2a[0], cot2b[0])
    lo, hi = pl.ds(0, 2), pl.ds(2, 2)
    up0, down0 = c0.at[lo, col(1)[1], c], c0.at[hi, col(3)[1], c]
    cot2a.append(push(piece.at[0], (up0, up0, at_y(1)[1]), (down0, down0, at_y(3)[1])))
    up1, down1 = c1.at[row(1)[0], lo, c], c1.at[row(3)[0], hi, c]
    cot2b.append(push(piece.at[0], (up1, up1, at_xc(1, 0)[2]), (down1, down1, at_xc(3, 0)[2])))
    to_partner(2, c0, col, (1, 3))
    to_partner(2, c1, row, (1, 3))

    z_wait(1, s["asend"])

    for b in range(BLOCKS):
        v = jnp.dot(tok(b), down_of(b), preferred_element_type=F32)
        lp[b // 2, 2 * (b % 2) : 2 * (b % 2) + 2] = v.astype(BF16).reshape(2, 2, ROWS, RANKS)

    lowx = push(
        s["lr"],
        *[
            (lp.at[at_xc(dx, dc)[0], :, at_xc(dx, dc)[1]], s["lr"].at[n], at_xc(dx, dc)[2])
            for n, (dx, dc) in enumerate(rows7)
        ],
    )
    z_send(2, s["gasend"], s["garecv"], 0, 9)

    arrived(cot2b[1], cot2a[1])
    to_partner(1, c1, row, (2,))
    to_partner(1, c0, col, (2,))

    def total(own, ref, n):
        v = own.astype(F32)
        for k in range(n):
            v = v + ref[k].astype(F32)
        return v

    arrived(lowx)
    s["lq"][...] = total(lp.at[x, :, c][...], s["lr"], 7).astype(BF16)
    lowy = push(
        s["ls"], *[(s["lq"].at[at_y(d)[0]], s["ls"].at[d - 1], at_y(d)[1]) for d in (1, 3, 2)]
    )
    rs1a.append(push(piece.at[0], *scatter_x((2,))))

    arrived(*cot3)

    for xx in range(NX):
        rows = NY * 2 * ROWS
        v = lax.dot_general(
            c0[xx].reshape(rows, HALF), s["wv"][:, :HALF], last, preferred_element_type=F32
        )
        v = v + lax.dot_general(
            c1[xx].reshape(rows, HALF), s["wv"][:, HALF:], last, preferred_element_type=F32
        )
        low = [
            lax.dot_general(s["lgm"][2 * xx + k], down_of(2 * xx + k), last, preferred_element_type=F32)
            for k in range(2)
        ]
        ig_o[xx] = (v + jnp.concatenate(low, axis=0)).astype(BF16)


    arrived(lowy)
    la[x, y, c] = total(s["lq"][y], s["ls"], 3).astype(BF16)
    lay = gather_y(la)
    arrived(lay)
    last_low = gather_x(la)
    arrived(*rs1a)
    for yy in range(NY):
        v = total(s["pa"][x, yy], s["ra1"].at[:, yy], 3)
        s["qa"][yy] = v.astype(BF16)
    rs2a = push(
        s["ra2"], *[(s["qa"].at[at_y(d)[0]], s["ra2"].at[d - 1], at_y(d)[1]) for d in (1, 3, 2)]
    )
    arrived(last_low)

    group = x * 8 + t
    chunk = pl.ds(pl.multiple_of(lax.rem(lax.div(group, 2), 8) * 128, 128), 128)
    values = lax.div(group, 16)

    def cot_cols(b):
        at = (b // 2, slice(2 * (b % 2), 2 * (b % 2) + 2), slice(None), slice(None), chunk)
        v = jnp.where(values == 0, c0[at].astype(F32), c1[at].astype(F32))
        return v.astype(BF16).reshape(4 * ROWS, 128)

    wide = lax.broadcasted_iota(I32, (COLS, 128), 1)

    def up_part(b):
        v = lax.dot_general(low_of(la, b), cot_cols(b), first, preferred_element_type=F32)
        v = jnp.where(values == 0, v[:COLS], v[COLS:])
        return v, pltpu.roll(v, COLS, 1)

    for b4 in range(4):
        lo, lo_r = up_part(b4)
        hi, hi_r = up_part(b4 + 4)
        left = jnp.where(c == 0, lo, lo_r)
        right = jnp.where(c == 0, hi_r, hi)
        v = jnp.where(wide < COLS, left, right)
        for k in range(NZ):
            s["gbf"][k, b4 * UP : (b4 + 1) * UP, :] = v[k * UP : (k + 1) * UP]
    s["gbsend"][...] = s["gbf"][...].astype(BF16)
    z_send(3, s["gbsend"], s["gbrecv"])
    z_send(2, s["gasend"], s["garecv"], 13, 15)
    s["gbrecv"][z] = s["gbsend"][z]

    arrived(*rs1b)
    for xx in range(NX):
        v = total(s["pb"][y, xx], s["rb1"].at[:, xx], 3)
        s["qb"][xx] = v.astype(BF16)
    rs2b = push(
        s["rb2"],
        *[(s["qb"].at[at_xc(d, 0)[0]], s["rb2"].at[d - 1], at_xc(d, 0)[2]) for d in (1, 3, 2)],
    )

    ids = lax.broadcasted_iota(I32, (SLOTS, NZ * BLOCKS), 0)
    sel = jnp.where(ids == s["tga"][...], 1.0, 0.0).astype(BF16)
    z_wait(2, s["gasend"])
    for r in range(DOWN):
        lanes = slice(r * RANKS, (r + 1) * RANKS)
        data = s["garecv"][:, :, lanes].astype(F32).reshape(NZ * BLOCKS, RANKS).astype(BF16)
        v = jnp.dot(sel, data, preferred_element_type=F32)
        ga_o[pl.ds(r, SLOTS, stride=DOWN), :] = v

    arrived(rs2a, rs2b, quad)
    low_rows = la[x, y, c]
    for j in range(4):
        cols = slice((j % 2) * QUARTER, (j % 2 + 1) * QUARTER)
        if j < 2:
            own, r1, r2 = s["pa"][x, y, :, cols], s["ra1"].at[:, y, :, cols], s["ra2"].at[:, :, cols]
        else:
            own, r1, r2 = s["pb"][y, x, :, cols], s["rb1"].at[:, x, :, cols], s["rb2"].at[:, :, cols]
        side = low_rows[:, :COLS] if j < 2 else low_rows[:, COLS:]
        v = total(total(own, r1, 3), r2, 3)
        v = v + jnp.dot(side, s["bown"][j], preferred_element_type=F32)
        kv_o[:, j * QUARTER : (j + 1) * QUARTER] = v.astype(BF16)

    z_wait(3, s["gbsend"])
    data = s["gbrecv"][...].reshape(NZ * DOWN, RANKS)
    ids = lax.broadcasted_iota(I32, (UP * SLOTS, NZ * DOWN), 0)
    sums = []
    for h in range(2):
        sel = jnp.where(ids == s["tgb"][h], 1.0, 0.0).astype(BF16)
        sums.append(jnp.dot(sel, data, preferred_element_type=F32))
    for i in range(UP):
        at = slice(i * SLOTS, (i + 1) * SLOTS)
        lo, hi = sums[0][at].T, sums[1][at].T
        gb_o[i] = lo[:COLS] + hi[COLS:]

    for i, like in enumerate(groups):
        until(like, s["ps"].at[i])
    for kind, name in enumerate(("bsend", "asend", "gasend", "gbsend")):
        until(s[name].at[pl.ds(0, NZ - 1)], s["zs"].at[kind])
    assert len(groups) == GROUPS, len(groups)

def write_out(kv, ig, ga, gb, kv_o, ig_o, ga_o, gb_o, sem):
    pairs = ((ga, ga_o), (ig, ig_o), (kv, kv_o), (gb, gb_o))
    copies = [pltpu.make_async_copy(v, o, sem.at[i]) for i, (v, o) in enumerate(pairs)]
    for cp in copies:
        cp.start()
    for cp in copies:
        cp.wait()


def body(tokens, weight, down, up, tenant_of_block, slot_of_tenant, cotangent):
    sc = scratches()
    anywhere = pl.BlockSpec(memory_space=pl.ANY)
    vmem = pl.BlockSpec(memory_space=pltpu.VMEM)
    results = (
        ((ROWS, WIDTH), BF16),
        ((NX, NY * 2 * ROWS, FEATS), BF16),
        ((SLOTS * DOWN, RANKS), F32),
        ((UP, COLS, SLOTS), F32),
    )
    kv, ig, ga, gb = pl.pallas_call(
        functools.partial(kern, tuple(sc)),
        out_shape=tuple(pltpu.VMEM(shape, kind) for shape, kind in results),
        in_specs=[anywhere] * 7,
        out_specs=(vmem,) * 4,
        scratch_shapes=list(sc.values()),
        compiler_params=pltpu.CompilerParams(
            collective_id=0, has_side_effects=True, vmem_limit_bytes=60 * 1024 * 1024
        ),
    )(
        tenant_of_block,
        slot_of_tenant,
        tokens.reshape(NX, NY, 2, ROWS, FEATS),
        weight,
        down,
        up,
        cotangent,
    )
    near = [pltpu.with_memory_space_constraint(v, pltpu.VMEM) for v in (kv, ig, ga, gb)]
    kv, ig, ga, gb = pl.pallas_call(
        write_out,
        out_shape=tuple(jax.ShapeDtypeStruct(shape, kind) for shape, kind in results),
        in_specs=[vmem] * 4,
        out_specs=(anywhere,) * 4,
        scratch_shapes=[pltpu.SemaphoreType.DMA((4,))],
    )(*near)
    return (
        kv,
        ig.reshape(NX * NY * 2 * ROWS, FEATS),
        ga.reshape(SLOTS, DOWN, RANKS),
        gb.transpose(2, 0, 1),
    )


def solution(mesh):
    placed = (
        P("dp", ("pipe", "tensor")),
        P(("pipe", "tensor"), None),
        P(None, ("pipe", "tensor", "dp"), None),
        P(None, "dp", None),
        P(),
        P(),
        P(("dp", "pipe", "tensor"), None),
    )
    return jax.shard_map(
        body,
        mesh=mesh,
        in_specs=placed,
        out_specs=(
            P(("dp", "pipe", "tensor"), None),
            P("dp", ("pipe", "tensor")),
            P(None, ("pipe", "tensor", "dp"), None),
            P(None, "dp", ("pipe", "tensor")),
        ),
        check_vma=False,
    )
```
